32 devices in a mesh: grp: 2 (over x), wide: 16 (over z, y, core).
Axes of the slice: x: 2, y: 2, z: 4, core: 2. Of those that a mesh axis runs over, the one named last changes fastest.
Arguments:
- query_rows: bfloat16 [2048, 2048], P(('grp', 'wide')), parts along dimension 0, may hold values from -10 to 10
- row_key_value: bfloat16 [2048, 512], P(('grp', 'wide')), parts along dimension 0, may hold values from -6 to 6
- key_value_cache: bfloat16 [65536, 512], P(('grp', 'wide')), parts along dimension 0, may hold values from -5 to 5
- resid: bfloat16 [2048, 2048], P(('grp', 'wide')), parts along dimension 0, may hold values from -12 to 12
- norm_gain: float32 [2048], replicated, may hold values from 0.5 to 1.5
- lengths: int32 [16], P('grp'), parts along dimension 0, may hold values from 1024 to 4096, as said below
- positions: int32 [16, 128], P('grp'), parts along dimension 0, may hold values from 0 to 4095, as said below
- expert_ids: int32 [2048, 8], P(('grp', 'wide')), parts along dimension 0, may hold values from 0 to 15, all different within a row; in each aligned block of 64 rows (0 to 63, 64 to 127, ...) at most 48 rows name the same one
- gate_scores: float32 [2048, 8], P(('grp', 'wide')), parts along dimension 0, may hold values from 0.1 to 1
- w_gate: bfloat16 [16, 2048, 768], P('wide'), may hold values from -0.125 to 0.125
- w_up: bfloat16 [16, 2048, 768], P('wide'), may hold values from -0.125 to 0.125
- w_down: bfloat16 [16, 768, 2048], P('wide'), may hold values from -0.21875 to 0.21875
Outputs:
- out_rows: bfloat16 [2048, 2048], P(('grp', 'wide')), parts along dimension 0
The draws below stay inside these ranges and needn't reach their ends.
There are 2 independent parts, one for each index of `grp`. The reference program is written for one: setup_inputs(seed, part) draws one part's arguments, and reference() takes and returns one part's arrays. A program takes and returns all parts, laid end to end along the dimension named above; an argument that names none is the same for every part. Nothing has to cross between parts.
Inputs may be any that keep to these rules, and one draw needn't show every extreme that they name: `lengths`: one document has length exactly 4096 and another exactly 1024. Within a document the positions are distinct and below its length. `expert_ids`: the 64 rows of one device name each expert at most 48 times, and some expert exactly that often.
All inputs are finite; a program needn't handle non-finite values.
Results may differ from the reference program's by a relative error of at most 0.0095.
Values may be sent and summed in bfloat16 or wider, within the bound.
No kernel may reach another device: no remote copies, remote signals or barrier semaphores. Data moves between devices by JAX's collectives and lax.ppermute only.
A program may use at most 128 MiB of HBM per device.

```python
import math
import jax
import jax.numpy as jnp
import numpy as np
from jax import lax

D = 2048
QUERY_HEADS = 32
KEY_VALUE_HEADS = 4
HEAD_SIZE = 64
FF = 768
TOP = 8
HALF_DOC_ROWS = 64
CACHED_POSITIONS = 2048
DOCUMENT_COUNT = 8
MASKED_ROWS = 1024
EXPERTS = 16
MOST = 48
N_WIDE = 16


def doc_layout(key):
    layout_key = jax.random.fold_in(key, 11)
    length_key, full_key, offset_key = jax.random.split(layout_key, 3)
    lengths = jax.random.randint(length_key, (DOCUMENT_COUNT,), CACHED_POSITIONS // 2, 2 * CACHED_POSITIONS + 1)
    full_doc = jax.random.randint(full_key, (), 0, DOCUMENT_COUNT)
    short_doc = (full_doc + 1) % DOCUMENT_COUNT
    doc_range = jnp.arange(DOCUMENT_COUNT)
    lengths = jnp.where(doc_range == full_doc, 2 * CACHED_POSITIONS, lengths)
    lengths = jnp.where(doc_range == short_doc, CACHED_POSITIONS // 2, lengths).astype(jnp.int32)
    stride = lengths // (2 * HALF_DOC_ROWS)
    offsets = jax.random.randint(offset_key, (DOCUMENT_COUNT, 2 * HALF_DOC_ROWS), 0, stride[:, None])
    slot_range = jnp.arange(2 * HALF_DOC_ROWS)
    is_full = (doc_range == full_doc)[:, None]
    offsets = jnp.where(is_full & (slot_range[None, :] == 0), 0, offsets)
    offsets = jnp.where(is_full & (slot_range[None, :] == 2 * HALF_DOC_ROWS - 1), stride[:, None] - 1, offsets)
    positions = slot_range[None, :].astype(jnp.int32) * stride[:, None] + offsets
    return (lengths, positions.astype(jnp.int32))


def draw_lengths(key, part):
    lengths, positions = doc_layout(key)
    return lengths


def draw_positions(key, part):
    lengths, positions = doc_layout(key)
    return positions


def draw_query_rows(key, part):
    subkey = jax.random.fold_in(key, 1)
    array_shape = (DOCUMENT_COUNT, 2 * HALF_DOC_ROWS, QUERY_HEADS * HEAD_SIZE)
    base_draw = jnp.clip(2.5 * jax.random.normal(subkey, array_shape, jnp.float32), -10.0, 10.0)
    return base_draw.reshape(MASKED_ROWS, QUERY_HEADS * HEAD_SIZE).astype(jnp.bfloat16)


def draw_row_key_value(key, part):
    key_draw, value_draw = jax.random.split(jax.random.fold_in(key, 2))
    array_shape = (DOCUMENT_COUNT, 2 * HALF_DOC_ROWS, KEY_VALUE_HEADS * HEAD_SIZE)
    key_portion = jnp.clip(1.6 * jax.random.normal(key_draw, array_shape, jnp.float32), -6.0, 6.0)
    value_portion = jnp.clip(jax.random.normal(value_draw, array_shape, jnp.float32), -5.0, 5.0)
    joined_parts = jnp.concatenate([key_portion, value_portion], axis=-1)
    return joined_parts.reshape(MASKED_ROWS, 2 * KEY_VALUE_HEADS * HEAD_SIZE).astype(jnp.bfloat16)


def draw_key_value_cache(key, part):
    base_key = jax.random.fold_in(jax.random.fold_in(key, 3), 0)
    array_shape = (DOCUMENT_COUNT * 2 * CACHED_POSITIONS, 2 * KEY_VALUE_HEADS * HEAD_SIZE)
    base_draw = jnp.clip(jax.random.normal(base_key, array_shape, jnp.float32), -5.0, 5.0)
    return base_draw.astype(jnp.bfloat16)


def draw_resid(key, part):
    base_key = jax.random.fold_in(jax.random.fold_in(key, 4), 0)
    array_shape = (MASKED_ROWS, D)
    base_draw = jnp.clip(jax.random.normal(base_key, array_shape, jnp.float32), -6.0, 6.0)
    return base_draw.astype(jnp.bfloat16)


def steps_of(rng, shape, cuts, least, high):
    loudness, own = 1.0, jax.random.fold_in(rng, 6)
    for position, blocks in cuts:
        heights = jnp.exp(jax.random.uniform(jax.random.fold_in(own, position), (blocks,), jnp.float32, least / len(cuts), high / len(cuts)))
        loudness = loudness * jnp.repeat(heights, shape[position] // blocks).reshape([-1 if axis == position else 1 for axis in range(len(shape))])
    return loudness


def assign_block(rng, own, number, rows, number_of, top, limit, slope):
    ranking = jax.random.permutation(rng, number_of)
    heavy_load, ordinary = portions_of(number_of, rows * top, limit, slope, True), portions_of(number_of, rows * top, limit, slope, False)
    places = jnp.arange(number_of)

    def named(sizes, offset_by):
        used = int((sizes > 0).sum())
        fixed = max(1, used // 4)
        passed = fixed + (places - fixed + offset_by * (used - fixed)) % max(1, number_of - fixed)
        return jnp.zeros((number_of,), jnp.int32).at[ranking[jnp.where(places < fixed, places, passed)]].set(jnp.asarray(sizes, jnp.int32))

    sizes = jnp.where(number % 4 == 0, named(heavy_load, number // 4), named(ordinary, number - number // 4 - 1))
    mixed = jax.random.permutation(jax.random.fold_in(own, 3), number_of)
    donor, receiver = mixed[0:number_of // 2 * 2:2], mixed[1:number_of // 2 * 2:2]
    room = jnp.minimum(sizes[donor] - 1, limit - sizes[receiver]) // 2
    room = jnp.where((donor == ranking[0]) | (receiver == ranking[0]) | (sizes[receiver] == 0), 0, jnp.maximum(room, 0))
    passed = jax.random.randint(jax.random.fold_in(own, 4), (number_of // 2,), 0, 1 << 20) % (room + 1)
    sizes = sizes.at[donor].add(-passed).at[receiver].add(passed)
    items = jnp.searchsorted(jnp.cumsum(sizes), jnp.arange(rows * top), side="right").astype(jnp.int32)
    table = items.reshape(top, rows).T
    table = table[jax.random.permutation(jax.random.fold_in(own, 1), rows)]
    offset_by = jax.random.randint(jax.random.fold_in(own, 2), (rows, 1), 0, top)
    return jnp.take_along_axis(table, (jnp.arange(top)[None, :] + offset_by) % top, axis=1)


def portions_of(amount, total, most, lean, full):
    portions = [(1 << 20) // math.isqrt(standing ** lean) + 1 for standing in range(1, amount + 1)]
    largest = most if full else min(most, max(-(-total // amount), total * portions[0] // sum(portions)))
    least = 1 if total - largest >= amount - 1 else 0
    given, spare = [largest] + [least] * (amount - 1), total - largest - least * (amount - 1)
    while spare > 0:
        free = [i for i in range(1, amount) if given[i] < largest] or [i for i in range(1, amount) if given[i] < most]
        pool, left = sum([portions[i] for i in free]), spare
        for i in free:
            extra = min(most - given[i], max(1, left * portions[i] // pool), spare)
            given[i] = given[i] + extra
            spare = spare - extra
    return np.array(given)


def gaussian(key, extent, deviation, most, cuts=(), kind=jnp.bfloat16):
    values = deviation * jax.random.normal(key, extent, jnp.float32)
    if cuts:
        values = values * steps_of(key, extent, cuts, -0.22, 0.18)
    return jnp.clip(values, -most, most).astype(kind)


def setup_inputs(seed: int = 0, part: int = 0) -> dict:
    streams_of = jax.random.split(jax.random.key(seed), 13)
    part_splits = jax.random.split(jax.random.fold_in(streams_of[12], part), 13)
    query_rows = draw_query_rows(jax.random.fold_in(jax.random.fold_in(streams_of[12], part), 71), part)
    row_key_value = draw_row_key_value(jax.random.fold_in(jax.random.fold_in(streams_of[12], part), 71), part)
    key_value_cache = draw_key_value_cache(jax.random.fold_in(jax.random.fold_in(streams_of[12], part), 71), part)
    resid = draw_resid(jax.random.fold_in(jax.random.fold_in(streams_of[12], part), 71), part)
    norm_gain = jnp.clip(1.0 + 0.1 * jax.random.normal(streams_of[4], (D,), jnp.float32), 0.5, 1.5)
    lengths = draw_lengths(jax.random.fold_in(jax.random.fold_in(streams_of[12], part), 71), part)
    positions = draw_positions(jax.random.fold_in(jax.random.fold_in(streams_of[12], part), 71), part)
    expert_ids_keys = jax.random.split(jax.random.fold_in(part_splits[7], 1), MASKED_ROWS // HALF_DOC_ROWS)
    expert_ids_turns = jax.random.permutation(jax.random.fold_in(part_splits[7], 3), MASKED_ROWS // HALF_DOC_ROWS)
    expert_ids = jax.vmap(lambda own, number: assign_block(jax.random.fold_in(part_splits[7], 2), own, number, HALF_DOC_ROWS, EXPERTS, TOP, MOST, 2))(expert_ids_keys, expert_ids_turns).reshape((MASKED_ROWS, TOP))
    gate_scores = jnp.clip(jnp.exp(math.log(1.0) - 2.3025851 * jax.random.uniform(part_splits[8], (MASKED_ROWS, TOP), jnp.float32) ** steps_of(part_splits[8], (MASKED_ROWS, TOP), ((0, 16),), -0.2, 0.2)), 0.1, 1.0)
    w_gate = gaussian(streams_of[9], (EXPERTS, D, FF), D ** -0.5, 0.125, ((0, 16),))
    w_up = gaussian(streams_of[10], (EXPERTS, D, FF), D ** -0.5, 0.125, ((0, 16),))
    w_down = gaussian(streams_of[11], (EXPERTS, FF, D), FF ** -0.5, 0.21875, ((0, 16),))
    return {"query_rows": query_rows, "row_key_value": row_key_value, "key_value_cache": key_value_cache, "resid": resid, "norm_gain": norm_gain, "lengths": lengths, "positions": positions, "expert_ids": expert_ids, "gate_scores": gate_scores, "w_gate": w_gate, "w_up": w_up, "w_down": w_down}


def single_document(element):
    query_tile_block, cache_rows, row_keys, length, marked = element
    key_value_width = KEY_VALUE_HEADS * HEAD_SIZE
    query_group_width = QUERY_HEADS // KEY_VALUE_HEADS
    document_rows = 2 * HALF_DOC_ROWS
    location = jnp.arange(2 * CACHED_POSITIONS, dtype=jnp.int32)
    is_marked = jnp.any(location[:, None] == marked[None, :].astype(jnp.int32), axis=1)
    usable = jnp.concatenate([(location < length.astype(jnp.int32)) & ~is_marked, jnp.ones((document_rows,), dtype=bool)])
    joined_parts = jnp.concatenate([cache_rows, row_keys], axis=0).astype(jnp.float32)
    key_portion = joined_parts[:, :key_value_width].reshape(-1, KEY_VALUE_HEADS, HEAD_SIZE)
    value_portion = joined_parts[:, key_value_width:].reshape(-1, KEY_VALUE_HEADS, HEAD_SIZE)
    query_head_rows = query_tile_block.astype(jnp.float32).reshape(document_rows, KEY_VALUE_HEADS, query_group_width, HEAD_SIZE)
    scores = jnp.einsum('mgqd,lgd->mgql', query_head_rows, key_portion, precision=lax.Precision.HIGHEST) * (1.0 / math.sqrt(HEAD_SIZE))
    scores = jnp.where(usable, scores, -1e+30)
    row_max = lax.optimization_barrier(jnp.max(scores, axis=-1, keepdims=True))
    weights = jnp.where(usable, jnp.exp(scores - row_max), 0.0)
    denominator = lax.optimization_barrier(jnp.sum(weights, axis=-1))
    rounded = lax.optimization_barrier(weights.astype(jnp.bfloat16)).astype(jnp.float32)
    summed = jnp.einsum('mgql,lgd->mgqd', rounded, value_portion, precision=lax.Precision.HIGHEST)
    attention_output = summed / denominator[..., None]
    return attention_output.reshape(document_rows, QUERY_HEADS * HEAD_SIZE).astype(jnp.bfloat16)

def reference(query_rows, row_key_value, key_value_cache, resid, norm_gain, lengths, positions, expert_ids, gate_scores, w_gate, w_up, w_down):
    document_rows = 2 * HALF_DOC_ROWS
    attention_output = lax.map(single_document, (query_rows.reshape(DOCUMENT_COUNT, document_rows, QUERY_HEADS * HEAD_SIZE), key_value_cache.reshape(DOCUMENT_COUNT, 2 * CACHED_POSITIONS, 2 * KEY_VALUE_HEADS * HEAD_SIZE), row_key_value.reshape(DOCUMENT_COUNT, document_rows, 2 * KEY_VALUE_HEADS * HEAD_SIZE), lengths, positions))
    attention_output = attention_output.reshape(MASKED_ROWS, QUERY_HEADS * HEAD_SIZE)
    residual = resid.astype(jnp.float32) + attention_output.astype(jnp.float32)
    normed = (residual * lax.rsqrt(lax.optimization_barrier(jnp.mean(residual * residual, axis=-1, keepdims=True)) + 1e-06) * norm_gain).astype(jnp.bfloat16)
    mix = gate_scores / lax.optimization_barrier(jnp.sum(gate_scores, axis=-1, keepdims=True))
    capacity = N_WIDE * MOST

    def one_expert(accumulator, expert_index):
        chosen = expert_ids == expert_index
        member = jnp.any(chosen, axis=-1)
        expert_share = lax.optimization_barrier(jnp.sum(jnp.where(chosen, mix, 0.0), axis=-1))
        gathered_order = jnp.argsort((~member).astype(jnp.int32), stable=True)[:capacity]
        picked = normed[gathered_order]
        gate_matrix = lax.dynamic_index_in_dim(w_gate, expert_index, 0, keepdims=False)
        up_matrix = lax.dynamic_index_in_dim(w_up, expert_index, 0, keepdims=False)
        down_matrix = lax.dynamic_index_in_dim(w_down, expert_index, 0, keepdims=False)
        gate_act = jnp.dot(picked, gate_matrix, preferred_element_type=jnp.float32)
        up_act = jnp.dot(picked, up_matrix, preferred_element_type=jnp.float32)
        hidden = (jax.nn.silu(gate_act) * up_act).astype(jnp.bfloat16)
        expert_out = jnp.dot(hidden, down_matrix, preferred_element_type=jnp.float32).astype(jnp.bfloat16)
        accumulator = accumulator.at[gathered_order].add(expert_share[gathered_order][:, None] * expert_out.astype(jnp.float32))
        return (accumulator, None)
    accumulator, unused = lax.scan(one_expert, jnp.zeros((MASKED_ROWS, D), jnp.float32), jnp.arange(EXPERTS, dtype=jnp.int32))
    return (residual + accumulator).astype(jnp.bfloat16)
```

```python
import math

import jax
import jax.numpy as jnp
from jax import lax
from jax.sharding import PartitionSpec as P

QUERY_HEADS = 32
KEY_VALUE_HEADS = 4
HEAD_SIZE = 64


score_masked_rows = -1e30


def swapped(shard, axis, bit):
    return lax.ppermute(shard, axis, [(i, i ^ 1 << bit) for i in range(lax.axis_size(axis))])


def exchanged(shard, axis, distance):
    return lax.ppermute(shard, axis, [(i, i ^ distance) for i in range(lax.axis_size(axis))])


def gather_planes(payload, axis, planes):
    blocks = []
    for k in range(planes):
        away = payload if k == 0 else exchanged(payload, axis, 4 * k)
        pair = jnp.concatenate([away, exchanged(away, axis, 2)], axis=0)
        blocks.append(jnp.concatenate([pair, exchanged(pair, axis, 1)], axis=0))
    return blocks


def scatter_planes(partials, axis):
    total = None
    for k, partial in enumerate(partials):
        rows = partial.shape[0] // 2
        half = partial[:rows] + exchanged(partial[rows:].astype(jnp.bfloat16), axis, 1).astype(jnp.float32)
        rows //= 2
        quarter = half[:rows] + exchanged(half[rows:].astype(jnp.bfloat16), axis, 2).astype(jnp.float32)
        if k:
            quarter = exchanged(quarter.astype(jnp.bfloat16), axis, 4 * k).astype(jnp.float32)
        total = quarter if total is None else total + quarter
    return total


def empty_state(masked_row_count):
    query_group_width = QUERY_HEADS // KEY_VALUE_HEADS
    return (
        jnp.zeros((masked_row_count, KEY_VALUE_HEADS, query_group_width, HEAD_SIZE), jnp.float32),
        jnp.full(
            (masked_row_count, KEY_VALUE_HEADS, query_group_width), score_masked_rows, jnp.float32
        ),
        jnp.zeros((masked_row_count, KEY_VALUE_HEADS, query_group_width), jnp.float32),
    )


def split_heads(query_matrix):
    return query_matrix.reshape(
        query_matrix.shape[0], KEY_VALUE_HEADS, QUERY_HEADS // KEY_VALUE_HEADS, HEAD_SIZE
    )


def attend_block(softmax_state, query_head_rows, key_tile_block, usable):
    accumulated, running_max, denominator = softmax_state
    key_value_width = KEY_VALUE_HEADS * HEAD_SIZE
    key_portion = key_tile_block[:, :key_value_width].reshape(
        key_tile_block.shape[0], KEY_VALUE_HEADS, HEAD_SIZE
    )
    value_portion = key_tile_block[:, key_value_width:].reshape(
        key_tile_block.shape[0], KEY_VALUE_HEADS, HEAD_SIZE
    )
    scores = jnp.einsum(
        "mgqd,lgd->mgql", query_head_rows, key_portion, preferred_element_type=jnp.float32
    ) * (1.0 / math.sqrt(HEAD_SIZE))
    if usable is not None:
        scores = jnp.where(usable, scores, score_masked_rows)
    new_max = jnp.maximum(running_max, jnp.max(scores, axis=-1))
    weights = jnp.exp(scores - new_max[..., None])
    if usable is not None:
        weights = jnp.where(usable, weights, 0.0)
    rescale = jnp.exp(running_max - new_max)
    denominator = denominator * rescale + jnp.sum(weights, axis=-1)
    accumulated = accumulated * rescale[..., None] + jnp.einsum(
        "mgql,lgd->mgqd",
        weights.astype(jnp.bfloat16),
        value_portion,
        preferred_element_type=jnp.float32,
    )
    return (accumulated, new_max, denominator)


def attend_cache(softmax_state, query_head_rows, cache_rows, start, length, marked):
    cache_span = cache_rows.shape[0]
    block_size = min(cache_span, 1024)
    block_count = cache_span // block_size
    blocks = cache_rows.reshape(block_count, block_size, cache_rows.shape[1])

    def cache_step(carried, element):
        block_index, key_tile_block = element
        location = start + block_index * block_size + jnp.arange(block_size, dtype=jnp.int32)
        is_marked = jnp.any(location[:, None] == marked[None, :], axis=1)
        usable = (location < length) & ~is_marked
        return (attend_block(carried, query_head_rows, key_tile_block, usable), None)

    softmax_state, unused = lax.scan(
        cache_step, softmax_state, (jnp.arange(block_count, dtype=jnp.int32), blocks)
    )
    return softmax_state


def local_part(query_matrix, row_key_value, key_value_cache, start, length, marked):
    query_head_rows = split_heads(query_matrix)
    softmax_state = attend_block(
        empty_state(query_matrix.shape[0]), query_head_rows, row_key_value, None
    )
    return attend_cache(softmax_state, query_head_rows, key_value_cache, start, length, marked)


def normalize_state(softmax_state, masked_row_count):
    accumulated, running_max, denominator = softmax_state
    return (
        (accumulated / denominator[..., None])
        .reshape(masked_row_count, QUERY_HEADS * HEAD_SIZE)
        .astype(jnp.bfloat16)
    )


def local(
    query_rows,
    row_key_value,
    key_value_cache,
    resid,
    norm_gain,
    lengths,
    positions,
    expert_ids,
    gate_scores,
    w_gate,
    w_up,
    w_down,
):
    masked_row_count = query_rows.shape[0]
    cache_span = key_value_cache.shape[0]
    query_group_width = QUERY_HEADS // KEY_VALUE_HEADS
    device = lax.axis_index("wide")
    doc_index = device // 2
    half_index = device % 2
    length = lax.dynamic_index_in_dim(lengths, doc_index, 0, keepdims=False)
    marked = lax.dynamic_index_in_dim(positions, doc_index, 0, keepdims=False)
    own_sum, own_max, own_total = local_part(
        query_rows, row_key_value, key_value_cache, half_index * cache_span, length, marked
    )
    visitor = swapped(query_rows, "wide", 0)
    hosted_sum, hosted_max, hosted_total = local_part(
        visitor, row_key_value, key_value_cache, half_index * cache_span, length, marked
    )
    far_sum, far_max, far_total = (
        swapped(
            hosted_sum.reshape(masked_row_count, QUERY_HEADS * HEAD_SIZE).astype(jnp.bfloat16),
            "wide",
            0,
        ).astype(jnp.float32),
        swapped(
            hosted_max.reshape(masked_row_count, QUERY_HEADS).astype(jnp.bfloat16), "wide", 0
        ).astype(jnp.float32),
        swapped(
            hosted_total.reshape(masked_row_count, QUERY_HEADS).astype(jnp.bfloat16), "wide", 0
        ).astype(jnp.float32),
    )
    far_sum = far_sum.reshape(masked_row_count, KEY_VALUE_HEADS, query_group_width, HEAD_SIZE)
    far_max = far_max.reshape(masked_row_count, KEY_VALUE_HEADS, query_group_width)
    far_total = far_total.reshape(masked_row_count, KEY_VALUE_HEADS, query_group_width)
    joint_max = jnp.maximum(own_max, far_max)
    own_scale = jnp.exp(own_max - joint_max)
    far_scale = jnp.exp(far_max - joint_max)
    merged_sum = own_sum * own_scale[..., None] + far_sum * far_scale[..., None]
    merged_total = own_total * own_scale + far_total * far_scale
    attention_output = normalize_state((merged_sum, joint_max, merged_total), masked_row_count)
    model_width = resid.shape[1]
    residual = resid.astype(jnp.float32) + attention_output.astype(jnp.float32)
    normed = (
        residual
        * lax.rsqrt(jnp.mean(residual * residual, axis=-1, keepdims=True) + 1e-06)
        * norm_gain
    ).astype(jnp.bfloat16)
    mix = gate_scores / jnp.sum(gate_scores, axis=-1, keepdims=True)
    experts = lax.axis_size("wide")
    shares = jnp.sum(
        jnp.where(expert_ids[..., None] == jnp.arange(experts, dtype=jnp.int32), mix[..., None], 0.0), axis=1
    )
    shares_high = shares.astype(jnp.bfloat16)
    shares_low = (shares - shares_high.astype(jnp.float32)).astype(jnp.bfloat16)
    tail = -(-2 * experts // 128) * 128
    filler = jnp.zeros((masked_row_count, tail - 2 * experts), jnp.bfloat16)
    payload = jnp.concatenate([normed, shares_high, shares_low, filler], axis=1)
    column = jnp.arange(tail, dtype=jnp.int32)
    own_column = ((column == device) | (column == device + experts)).astype(jnp.float32)
    partials = []
    for block in gather_planes(payload, "wide", experts // 4):
        rows = block[:, :model_width]
        share = jnp.sum(block[:, model_width:].astype(jnp.float32) * own_column, axis=1, keepdims=True)
        gate_act = jnp.dot(rows, w_gate[0], preferred_element_type=jnp.float32)
        up_act = jnp.dot(rows, w_up[0], preferred_element_type=jnp.float32)
        hidden = (jax.nn.silu(gate_act) * up_act).astype(jnp.bfloat16)
        expert_out = jnp.dot(hidden, w_down[0], preferred_element_type=jnp.float32).astype(jnp.bfloat16)
        partials.append(share * expert_out.astype(jnp.float32))
    routed_sum = scatter_planes(partials, "wide")
    return (residual + routed_sum).astype(jnp.bfloat16)


def solution(mesh):
    return jax.shard_map(
        local,
        mesh=mesh,
        in_specs=(
            P(("grp", "wide"), None),
            P(("grp", "wide"), None),
            P(("grp", "wide"), None),
            P(("grp", "wide"), None),
            P(),
            P("grp"),
            P("grp", None),
            P(("grp", "wide"), None),
            P(("grp", "wide"), None),
            P("wide", None, None),
            P("wide", None, None),
            P("wide", None, None),
        ),
        out_specs=P(("grp", "wide"), None),
        check_vma=False,
    )
```

```python
import math

import jax
import jax.numpy as jnp
from jax import lax
from jax.experimental import pallas as pl
from jax.experimental.pallas import tpu as pltpu
from jax.sharding import PartitionSpec as P

QUERY_HEADS = 32
KEY_VALUE_HEADS = 4
HEAD_SIZE = 64


score_masked_rows = -1e30


def exchanged(shard, axis, distance):
    return lax.ppermute(shard, axis, [(i, i ^ distance) for i in range(lax.axis_size(axis))])


def gather_planes(payload, axis, planes):
    blocks = []
    for k in range(planes):
        away = payload if k == 0 else exchanged(payload, axis, 4 * k)
        pair = jnp.concatenate([away, exchanged(away, axis, 2)], axis=0)
        blocks.append(jnp.concatenate([pair, exchanged(pair, axis, 1)], axis=0))
    return blocks


def scatter_planes(partials, axis):
    total = None
    for k, partial in enumerate(partials):
        rows = partial.shape[0] // 2
        half = partial[:rows] + exchanged(partial[rows:].astype(jnp.bfloat16), axis, 1).astype(jnp.float32)
        rows //= 2
        quarter = half[:rows] + exchanged(half[rows:].astype(jnp.bfloat16), axis, 2).astype(jnp.float32)
        if k:
            quarter = exchanged(quarter.astype(jnp.bfloat16), axis, 4 * k).astype(jnp.float32)
        total = quarter if total is None else total + quarter
    return total


LANES = 128


def cache_kernel(
    device_ref, lengths_ref, positions_ref, own_ref, visit_ref, row_k_ref, row_v_ref, cache_k_ref, cache_v_ref,
    own_out_ref, own_stats_ref, visit_out_ref,
    keys, values, stacked, result, shifts, stats,
):
    group = pl.program_id(0)
    rows = own_ref.shape[0]
    span = cache_k_ref.shape[0]
    pairs = own_ref.shape[1] // LANES
    key_count = keys.shape[0]
    padded = key_count - span
    lane = lax.broadcasted_iota(jnp.int32, (1, LANES), 1)

    @pl.when(group == 0)
    def _():
        device = device_ref[0]
        start = (device % 2) * span
        length = lengths_ref[device // 2]
        marked = positions_ref[pl.ds(device // 2, 1), :]
        counter = jnp.ones((marked.shape[1], LANES), jnp.bfloat16)
        step = LANES

        def mark(block, carry):
            location = start + block * step + lax.broadcasted_iota(jnp.int32, (step, 1), 0)
            equal = jnp.where(location == marked, 1.0, 0.0).astype(jnp.bfloat16)
            count = jnp.dot(equal, counter, preferred_element_type=jnp.float32)
            closed = ((count > 0.5) | (location >= length)) & (lane == 0)
            at = pl.ds(pl.multiple_of(block * step, step), step)
            keys[at, LANES:] = jnp.where(closed, score_masked_rows, 0.0).astype(jnp.bfloat16)
            values[at, LANES:] = jnp.ones((step, LANES), jnp.bfloat16)
            return carry

        lax.fori_loop(0, span // step, mark, 0)
        beyond = lax.broadcasted_iota(jnp.int32, (padded, 1), 0) >= rows
        keys[span:, LANES:] = jnp.where(beyond & (lane == 0), score_masked_rows, 0.0).astype(jnp.bfloat16)
        values[span:, LANES:] = jnp.ones((padded, LANES), jnp.bfloat16)
        stacked[:, LANES:] = jnp.where(
            lax.broadcasted_iota(jnp.int32, (stacked.shape[0], LANES), 1) == 0, 1.0, 0.0
        ).astype(jnp.bfloat16)
        stats[...] = jnp.zeros_like(stats)
        if padded > rows:
            keys[span + rows :, :LANES] = jnp.zeros((padded - rows, LANES), jnp.bfloat16)
            values[span + rows :, :LANES] = jnp.zeros((padded - rows, LANES), jnp.bfloat16)

    low = (lane < HEAD_SIZE) == (group % 2 == 0)

    def doubled(block):
        wide = block.astype(jnp.float32)
        return jnp.where(low, wide, pltpu.roll(wide, HEAD_SIZE, 1)).astype(jnp.bfloat16)

    keys[:span, :LANES] = doubled(cache_k_ref[...])
    values[:span, :LANES] = doubled(cache_v_ref[...])
    keys[span : span + rows, :LANES] = doubled(row_k_ref[...])
    values[span : span + rows, :LANES] = doubled(row_v_ref[...])
    scale = 1.0 / math.sqrt(HEAD_SIZE)
    for pair in range(pairs):
        for source, ref in enumerate((own_ref, visit_ref)):
            query = ref[:, pair * LANES : (pair + 1) * LANES].astype(jnp.float32) * scale
            for parity in range(2):
                base = ((parity * pairs + pair) * 2 + source) * rows
                kept = jnp.where((lane < HEAD_SIZE) == (parity == 0), query, 0.0)
                stacked[base : base + rows, :LANES] = kept.astype(jnp.bfloat16)

    chunk = 2 * rows
    for begin in range(0, stacked.shape[0], chunk):
        at = slice(begin, begin + chunk)
        scores = lax.dot_general(
            stacked[at, :], keys[...], (((1,), (1,)), ((), ())), preferred_element_type=jnp.float32
        )
        shift = jnp.max(scores, axis=1, keepdims=True).astype(jnp.bfloat16).astype(jnp.float32)
        weights = jnp.exp(scores - shift).astype(jnp.bfloat16)
        result[at, :] = jnp.dot(weights, values[...], preferred_element_type=jnp.float32)
        shifts[at, :] = jnp.broadcast_to(shift, (chunk, LANES))

    seen = stats[...]
    for pair in range(pairs):
        even = slice(pair * chunk, (pair + 1) * chunk)
        odd = slice((pairs + pair) * chunk, (pairs + pair + 1) * chunk)
        joined = jnp.where(lane < HEAD_SIZE, result[even, :LANES], result[odd, :LANES])
        own_out_ref[:, pair * LANES : (pair + 1) * LANES] = joined[:rows]
        column = pl.multiple_of((group * pairs + pair) * LANES, LANES)
        visit_out_ref[:, pl.ds(column, LANES)] = joined[rows:].astype(jnp.bfloat16)
        for parity, at in enumerate((even, odd)):
            head = (group * pairs + pair) * 2 + parity
            total = result[at, LANES:]
            high = total.astype(jnp.bfloat16).astype(jnp.float32)
            seen = jnp.where(lane == head, shifts[at, :], seen)
            seen = jnp.where(lane == head + QUERY_HEADS, high, seen)
            seen = jnp.where(lane == head + 2 * QUERY_HEADS, total - high, seen)
    stats[...] = seen

    @pl.when(group == pl.num_programs(0) - 1)
    def _():
        own_stats_ref[...] = stats[:rows].astype(jnp.bfloat16)
        visit_out_ref[:, visit_out_ref.shape[1] - LANES :] = stats[rows:].astype(jnp.bfloat16)


def attend_cache(device, lengths, positions, own, visit, row_key_value, key_value_cache):
    rows, width = own.shape
    span = key_value_cache.shape[0]
    key_count = span + -(-rows // LANES) * LANES
    group_width = width // KEY_VALUE_HEADS
    stack = 2 * rows * (QUERY_HEADS // KEY_VALUE_HEADS)
    half = KEY_VALUE_HEADS * HEAD_SIZE // LANES
    per_block = LANES // HEAD_SIZE
    return pl.pallas_call(
        cache_kernel,
        grid=(KEY_VALUE_HEADS,),
        in_specs=[
            pl.BlockSpec(memory_space=pltpu.SMEM),
            pl.BlockSpec(memory_space=pltpu.SMEM),
            pl.BlockSpec(positions.shape, lambda g: (0, 0)),
            pl.BlockSpec((rows, group_width), lambda g: (0, g)),
            pl.BlockSpec((rows, group_width), lambda g: (0, g)),
            pl.BlockSpec((rows, LANES), lambda g: (0, g // per_block)),
            pl.BlockSpec((rows, LANES), lambda g: (0, half + g // per_block)),
            pl.BlockSpec((span, LANES), lambda g: (0, g // per_block)),
            pl.BlockSpec((span, LANES), lambda g: (0, half + g // per_block)),
        ],
        out_specs=[
            pl.BlockSpec((rows, group_width), lambda g: (0, g)),
            pl.BlockSpec((rows, LANES), lambda g: (0, 0)),
            pl.BlockSpec((rows, width + LANES), lambda g: (0, 0)),
        ],
        out_shape=[
            jax.ShapeDtypeStruct((rows, width), jnp.float32),
            jax.ShapeDtypeStruct((rows, LANES), jnp.bfloat16),
            jax.ShapeDtypeStruct((rows, width + LANES), jnp.bfloat16),
        ],
        scratch_shapes=[
            pltpu.VMEM((key_count, 2 * LANES), jnp.bfloat16),
            pltpu.VMEM((key_count, 2 * LANES), jnp.bfloat16),
            pltpu.VMEM((stack, 2 * LANES), jnp.bfloat16),
            pltpu.VMEM((stack, 2 * LANES), jnp.float32),
            pltpu.VMEM((stack, LANES), jnp.float32),
            pltpu.VMEM((2 * rows, LANES), jnp.float32),
        ],
        name="cache_attention",
    )(
        device.reshape(1), lengths, positions, own, visit,
        row_key_value, row_key_value, key_value_cache, key_value_cache,
    )


def merge_kernel(own_ref, own_stats_ref, far_ref, resid_ref, gain_ref, shares_ref, payload_ref, residual_ref):
    width = own_ref.shape[1]
    far_stats = far_ref[:, width:]
    head_of = lax.broadcasted_iota(jnp.int32, (LANES, width), 1) // HEAD_SIZE
    stat = lax.broadcasted_iota(jnp.int32, (LANES, width), 0)

    def spread(stats):
        pick_shift = jnp.where(stat == head_of, 1.0, 0.0).astype(jnp.bfloat16)
        pick_total = jnp.where(
            (stat == head_of + QUERY_HEADS) | (stat == head_of + 2 * QUERY_HEADS), 1.0, 0.0
        ).astype(jnp.bfloat16)
        return (
            jnp.dot(stats, pick_shift, preferred_element_type=jnp.float32),
            jnp.dot(stats, pick_total, preferred_element_type=jnp.float32),
        )

    own_shift, own_total = spread(own_stats_ref[...])
    far_shift, far_total = spread(far_stats)
    joint = jnp.maximum(own_shift, far_shift)
    own_scale = jnp.exp(own_shift - joint)
    far_scale = jnp.exp(far_shift - joint)
    merged = own_ref[...] * own_scale + far_ref[:, :width].astype(jnp.float32) * far_scale
    total = own_total * own_scale + far_total * far_scale
    attn = (merged / total).astype(jnp.bfloat16).astype(jnp.float32)
    residual = resid_ref[...].astype(jnp.float32) + attn
    residual_ref[...] = residual
    power = jnp.mean(residual * residual, axis=1, keepdims=True)
    normed = residual * lax.rsqrt(power + 1e-06) * gain_ref[...]
    payload_ref[:, :width] = normed.astype(jnp.bfloat16)
    payload_ref[:, width:] = shares_ref[...]


def merge(own, own_stats, far, resid, norm_gain, shares):
    rows, width = own.shape
    return pl.pallas_call(
        merge_kernel,
        out_shape=[
            jax.ShapeDtypeStruct((rows, width + shares.shape[1]), jnp.bfloat16),
            jax.ShapeDtypeStruct((rows, width), jnp.float32),
        ],
        name="merge_norm",
    )(own, own_stats, far, resid, norm_gain.reshape(1, width), shares)


def local(
    query_rows,
    row_key_value,
    key_value_cache,
    resid,
    norm_gain,
    lengths,
    positions,
    expert_ids,
    gate_scores,
    w_gate,
    w_up,
    w_down,
):
    masked_row_count, model_width = resid.shape
    device = lax.axis_index("wide")
    experts = lax.axis_size("wide")
    mix = gate_scores / jnp.sum(gate_scores, axis=-1, keepdims=True)
    shares = jnp.sum(
        jnp.where(expert_ids[..., None] == jnp.arange(experts, dtype=jnp.int32), mix[..., None], 0.0), axis=1
    )
    shares_high = shares.astype(jnp.bfloat16)
    shares_low = (shares - shares_high.astype(jnp.float32)).astype(jnp.bfloat16)
    tail = -(-2 * experts // LANES) * LANES
    filler = jnp.zeros((masked_row_count, tail - 2 * experts), jnp.bfloat16)
    shares = jnp.concatenate([shares_high, shares_low, filler], axis=1)
    visitor = exchanged(query_rows, "wide", 1)
    own, own_stats, hosted = attend_cache(
        device, lengths, positions, query_rows, visitor, row_key_value, key_value_cache
    )
    far = exchanged(hosted, "wide", 1)
    payload, residual = merge(own, own_stats, far, resid, norm_gain, shares)
    column = jnp.arange(tail, dtype=jnp.int32)
    own_column = ((column == device) | (column == device + experts)).astype(jnp.float32)
    partials = []
    for block in gather_planes(payload, "wide", experts // 4):
        rows = block[:, :model_width]
        share = jnp.sum(block[:, model_width:].astype(jnp.float32) * own_column, axis=1, keepdims=True)
        gate_act = jnp.dot(rows, w_gate[0], preferred_element_type=jnp.float32)
        up_act = jnp.dot(rows, w_up[0], preferred_element_type=jnp.float32)
        hidden = (jax.nn.silu(gate_act) * up_act).astype(jnp.bfloat16)
        expert_out = jnp.dot(hidden, w_down[0], preferred_element_type=jnp.float32).astype(jnp.bfloat16)
        partials.append(share * expert_out.astype(jnp.float32))
    routed_sum = scatter_planes(partials, "wide")
    return (residual + routed_sum).astype(jnp.bfloat16)


def solution(mesh):
    return jax.shard_map(
        local,
        mesh=mesh,
        in_specs=(
            P(("grp", "wide"), None),
            P(("grp", "wide"), None),
            P(("grp", "wide"), None),
            P(("grp", "wide"), None),
            P(),
            P("grp"),
            P("grp", None),
            P(("grp", "wide"), None),
            P(("grp", "wide"), None),
            P("wide", None, None),
            P("wide", None, None),
            P("wide", None, None),
        ),
        out_specs=P(("grp", "wide"), None),
        check_vma=False,
    )
```

```python
import functools
import math

import jax
import jax.numpy as jnp
from jax import lax
from jax.experimental import pallas as pl
from jax.experimental.pallas import tpu as pltpu
from jax.sharding import PartitionSpec as P

QUERY_HEADS = 32
KEY_VALUE_HEADS = 4
HEAD_SIZE = 64


score_masked_rows = -1e30


def exchanged(shard, axis, distance):
    return lax.ppermute(shard, axis, [(i, i ^ distance) for i in range(lax.axis_size(axis))])


def after(value, *others):
    return lax.optimization_barrier((value, *others))[0]


LANES = 128


def cache_kernel(
    device_ref, lengths_ref, positions_ref, own_ref, visit_ref, row_k_ref, row_v_ref, cache_k_ref, cache_v_ref,
    own_out_ref, own_stats_ref, visit_out_ref,
    keys, values, stacked, result, shifts, stats,
):
    group = pl.program_id(0)
    rows = own_ref.shape[0]
    span = cache_k_ref.shape[0]
    pairs = own_ref.shape[1] // LANES
    key_count = keys.shape[0]
    padded = key_count - span
    lane = lax.broadcasted_iota(jnp.int32, (1, LANES), 1)

    @pl.when(group == 0)
    def _():
        device = device_ref[0]
        start = (device % 2) * span
        length = lengths_ref[device // 2]
        marked = positions_ref[pl.ds(device // 2, 1), :]
        counter = jnp.ones((marked.shape[1], LANES), jnp.bfloat16)
        step = LANES

        def mark(block, carry):
            location = start + block * step + lax.broadcasted_iota(jnp.int32, (step, 1), 0)
            equal = jnp.where(location == marked, 1.0, 0.0).astype(jnp.bfloat16)
            count = jnp.dot(equal, counter, preferred_element_type=jnp.float32)
            closed = ((count > 0.5) | (location >= length)) & (lane == 0)
            at = pl.ds(pl.multiple_of(block * step, step), step)
            keys[at, LANES:] = jnp.where(closed, score_masked_rows, 0.0).astype(jnp.bfloat16)
            values[at, LANES:] = jnp.ones((step, LANES), jnp.bfloat16)
            return carry

        lax.fori_loop(0, span // step, mark, 0)
        beyond = lax.broadcasted_iota(jnp.int32, (padded, 1), 0) >= rows
        keys[span:, LANES:] = jnp.where(beyond & (lane == 0), score_masked_rows, 0.0).astype(jnp.bfloat16)
        values[span:, LANES:] = jnp.ones((padded, LANES), jnp.bfloat16)
        stacked[:, LANES:] = jnp.where(
            lax.broadcasted_iota(jnp.int32, (stacked.shape[0], LANES), 1) == 0, 1.0, 0.0
        ).astype(jnp.bfloat16)
        stats[...] = jnp.zeros_like(stats)
        if padded > rows:
            keys[span + rows :, :LANES] = jnp.zeros((padded - rows, LANES), jnp.bfloat16)
            values[span + rows :, :LANES] = jnp.zeros((padded - rows, LANES), jnp.bfloat16)

    low = (lane < HEAD_SIZE) == (group % 2 == 0)

    def doubled(block):
        wide = block.astype(jnp.float32)
        return jnp.where(low, wide, pltpu.roll(wide, HEAD_SIZE, 1)).astype(jnp.bfloat16)

    keys[:span, :LANES] = doubled(cache_k_ref[...])
    values[:span, :LANES] = doubled(cache_v_ref[...])
    keys[span : span + rows, :LANES] = doubled(row_k_ref[...])
    values[span : span + rows, :LANES] = doubled(row_v_ref[...])
    scale = 1.0 / math.sqrt(HEAD_SIZE)
    for pair in range(pairs):
        for source, ref in enumerate((own_ref, visit_ref)):
            query = ref[:, pair * LANES : (pair + 1) * LANES].astype(jnp.float32) * scale
            for parity in range(2):
                base = ((parity * pairs + pair) * 2 + source) * rows
                kept = jnp.where((lane < HEAD_SIZE) == (parity == 0), query, 0.0)
                stacked[base : base + rows, :LANES] = kept.astype(jnp.bfloat16)

    chunk = 2 * rows
    for begin in range(0, stacked.shape[0], chunk):
        at = slice(begin, begin + chunk)
        scores = lax.dot_general(
            stacked[at, :], keys[...], (((1,), (1,)), ((), ())), preferred_element_type=jnp.float32
        )
        shift = jnp.max(scores, axis=1, keepdims=True).astype(jnp.bfloat16).astype(jnp.float32)
        weights = jnp.exp(scores - shift).astype(jnp.bfloat16)
        result[at, :] = jnp.dot(weights, values[...], preferred_element_type=jnp.float32)
        shifts[at, :] = jnp.broadcast_to(shift, (chunk, LANES))

    seen = stats[...]
    for pair in range(pairs):
        even = slice(pair * chunk, (pair + 1) * chunk)
        odd = slice((pairs + pair) * chunk, (pairs + pair + 1) * chunk)
        joined = jnp.where(lane < HEAD_SIZE, result[even, :LANES], result[odd, :LANES])
        own_out_ref[:, pair * LANES : (pair + 1) * LANES] = joined[:rows]
        column = pl.multiple_of((group * pairs + pair) * LANES, LANES)
        visit_out_ref[:, pl.ds(column, LANES)] = joined[rows:].astype(jnp.bfloat16)
        for parity, at in enumerate((even, odd)):
            head = (group * pairs + pair) * 2 + parity
            total = result[at, LANES:]
            high = total.astype(jnp.bfloat16).astype(jnp.float32)
            seen = jnp.where(lane == head, shifts[at, :], seen)
            seen = jnp.where(lane == head + QUERY_HEADS, high, seen)
            seen = jnp.where(lane == head + 2 * QUERY_HEADS, total - high, seen)
    stats[...] = seen

    @pl.when(group == pl.num_programs(0) - 1)
    def _():
        own_stats_ref[...] = stats[:rows].astype(jnp.bfloat16)
        visit_out_ref[:, visit_out_ref.shape[1] - LANES :] = stats[rows:].astype(jnp.bfloat16)


def attend_cache(device, lengths, positions, own, visit, row_key_value, key_value_cache):
    rows, width = own.shape
    span = key_value_cache.shape[0]
    key_count = span + -(-rows // LANES) * LANES
    group_width = width // KEY_VALUE_HEADS
    stack = 2 * rows * (QUERY_HEADS // KEY_VALUE_HEADS)
    half = KEY_VALUE_HEADS * HEAD_SIZE // LANES
    per_block = LANES // HEAD_SIZE
    return pl.pallas_call(
        cache_kernel,
        grid=(KEY_VALUE_HEADS,),
        in_specs=[
            pl.BlockSpec(memory_space=pltpu.SMEM),
            pl.BlockSpec(memory_space=pltpu.SMEM),
            pl.BlockSpec(positions.shape, lambda g: (0, 0)),
            pl.BlockSpec((rows, group_width), lambda g: (0, g)),
            pl.BlockSpec((rows, group_width), lambda g: (0, g)),
            pl.BlockSpec((rows, LANES), lambda g: (0, g // per_block)),
            pl.BlockSpec((rows, LANES), lambda g: (0, half + g // per_block)),
            pl.BlockSpec((span, LANES), lambda g: (0, g // per_block)),
            pl.BlockSpec((span, LANES), lambda g: (0, half + g // per_block)),
        ],
        out_specs=[
            pl.BlockSpec((rows, group_width), lambda g: (0, g)),
            pl.BlockSpec((rows, LANES), lambda g: (0, 0)),
            pl.BlockSpec((rows, width + LANES), lambda g: (0, 0)),
        ],
        out_shape=[
            jax.ShapeDtypeStruct((rows, width), jnp.float32),
            jax.ShapeDtypeStruct((rows, LANES), jnp.bfloat16),
            jax.ShapeDtypeStruct((rows, width + LANES), jnp.bfloat16),
        ],
        scratch_shapes=[
            pltpu.VMEM((key_count, 2 * LANES), jnp.bfloat16),
            pltpu.VMEM((key_count, 2 * LANES), jnp.bfloat16),
            pltpu.VMEM((stack, 2 * LANES), jnp.bfloat16),
            pltpu.VMEM((stack, 2 * LANES), jnp.float32),
            pltpu.VMEM((stack, LANES), jnp.float32),
            pltpu.VMEM((2 * rows, LANES), jnp.float32),
        ],
        compiler_params=pltpu.CompilerParams(vmem_limit_bytes=20 << 20),
        name="cache_attention",
    )(
        device.reshape(1), lengths, positions, own, visit,
        row_key_value, row_key_value, key_value_cache, key_value_cache,
    )


def merge_kernel(own_ref, own_stats_ref, far_ref, resid_ref, gain_ref, shares_ref, payload_ref, residual_ref):
    width = own_ref.shape[1]
    far_stats = far_ref[:, width:]
    head_of = lax.broadcasted_iota(jnp.int32, (LANES, width), 1) // HEAD_SIZE
    stat = lax.broadcasted_iota(jnp.int32, (LANES, width), 0)

    def spread(stats):
        pick_shift = jnp.where(stat == head_of, 1.0, 0.0).astype(jnp.bfloat16)
        pick_total = jnp.where(
            (stat == head_of + QUERY_HEADS) | (stat == head_of + 2 * QUERY_HEADS), 1.0, 0.0
        ).astype(jnp.bfloat16)
        return (
            jnp.dot(stats, pick_shift, preferred_element_type=jnp.float32),
            jnp.dot(stats, pick_total, preferred_element_type=jnp.float32),
        )

    own_shift, own_total = spread(own_stats_ref[...])
    far_shift, far_total = spread(far_stats)
    joint = jnp.maximum(own_shift, far_shift)
    own_scale = jnp.exp(own_shift - joint)
    far_scale = jnp.exp(far_shift - joint)
    merged = own_ref[...] * own_scale + far_ref[:, :width].astype(jnp.float32) * far_scale
    total = own_total * own_scale + far_total * far_scale
    attn = (merged / total).astype(jnp.bfloat16).astype(jnp.float32)
    residual = resid_ref[...].astype(jnp.float32) + attn
    residual_ref[...] = residual
    power = jnp.mean(residual * residual, axis=1, keepdims=True)
    normed = residual * lax.rsqrt(power + 1e-06) * gain_ref[...]
    payload_ref[:, :width] = normed.astype(jnp.bfloat16)
    payload_ref[:, width:] = shares_ref[...]


def merge(own, own_stats, far, resid, norm_gain, shares):
    rows, width = own.shape
    return pl.pallas_call(
        merge_kernel,
        out_shape=[
            jax.ShapeDtypeStruct((rows, width + shares.shape[1]), jnp.bfloat16),
            jax.ShapeDtypeStruct((rows, width), jnp.float32),
        ],
        compiler_params=pltpu.CompilerParams(vmem_limit_bytes=12 << 20),
        name="merge_norm",
    )(own, own_stats, far, resid, norm_gain.reshape(1, width), shares)


def expert_kernel(device_ref, near_ref, far_ref, gate_ref, up_ref, down_ref, keep_ref, send_ref, *, experts):
    depth = gate_ref.shape[1]
    hidden_width = gate_ref.shape[2]
    rows = jnp.concatenate([near_ref[...], far_ref[...]], axis=0)
    device = device_ref[0]
    column = lax.broadcasted_iota(jnp.int32, (1, rows.shape[1] - depth), 1)
    own_column = (column == device) | (column == device + experts)
    share = jnp.sum(
        jnp.where(own_column, rows[:, depth:].astype(jnp.float32), 0.0), axis=1, keepdims=True
    )
    rows = rows[:, :depth]
    step = 256
    hidden = []
    for begin in range(0, hidden_width, step):
        at = slice(begin, min(begin + step, hidden_width))
        gate_act = jnp.dot(rows, gate_ref[0, :, at], preferred_element_type=jnp.float32)
        up_act = jnp.dot(rows, up_ref[0, :, at], preferred_element_type=jnp.float32)
        hidden.append((jax.nn.silu(gate_act) * up_act).astype(jnp.bfloat16))
    hidden = jnp.concatenate(hidden, axis=1)
    kept = keep_ref.shape[0]
    step = 512
    for begin in range(0, depth, step):
        at = slice(begin, min(begin + step, depth))
        expert_out = jnp.dot(hidden, down_ref[0, :, at], preferred_element_type=jnp.float32)
        partial = share * expert_out.astype(jnp.bfloat16).astype(jnp.float32)
        keep_ref[:, at] = partial[:kept]
        send_ref[:, at] = partial[kept:].astype(jnp.bfloat16)


def expert(device, near, far, w_gate, w_up, w_down, experts):
    rows = near.shape[0]
    depth = w_gate.shape[1]
    return pl.pallas_call(
        functools.partial(expert_kernel, experts=experts),
        in_specs=[pl.BlockSpec(memory_space=pltpu.SMEM)] + [pl.BlockSpec(memory_space=pltpu.VMEM)] * 5,
        out_specs=[pl.BlockSpec(memory_space=pltpu.VMEM)] * 2,
        out_shape=[
            jax.ShapeDtypeStruct((rows, depth), jnp.float32),
            jax.ShapeDtypeStruct((rows, depth), jnp.bfloat16),
        ],
        compiler_params=pltpu.CompilerParams(vmem_limit_bytes=20 << 20),
        name="expert",
    )(device.reshape(1), near, far, w_gate, w_up, w_down)


def local(
    query_rows,
    row_key_value,
    key_value_cache,
    resid,
    norm_gain,
    lengths,
    positions,
    expert_ids,
    gate_scores,
    w_gate,
    w_up,
    w_down,
):
    masked_row_count, model_width = resid.shape
    device = lax.axis_index("wide")
    experts = lax.axis_size("wide")
    mix = gate_scores / jnp.sum(gate_scores, axis=-1, keepdims=True)
    shares = jnp.sum(
        jnp.where(expert_ids[..., None] == jnp.arange(experts, dtype=jnp.int32), mix[..., None], 0.0), axis=1
    )
    shares_high = shares.astype(jnp.bfloat16)
    shares_low = (shares - shares_high.astype(jnp.float32)).astype(jnp.bfloat16)
    tail = -(-2 * experts // LANES) * LANES
    filler = jnp.zeros((masked_row_count, tail - 2 * experts), jnp.bfloat16)
    shares = jnp.concatenate([shares_high, shares_low, filler], axis=1)
    visitor = exchanged(query_rows, "wide", 1)
    own, own_stats, hosted = attend_cache(
        device, lengths, positions, query_rows, visitor, row_key_value, key_value_cache
    )
    far = exchanged(hosted, "wide", 1)
    payload, residual = merge(own, own_stats, far, resid, norm_gain, shares)
    total = residual
    previous, ready = [], []
    for k in range(experts // 4):
        away = payload if k == 0 else exchanged(payload, "wide", 4 * k)
        if k > 1:
            away = after(away, previous[k - 2])
        near = jnp.concatenate([away, exchanged(away, "wide", 2)], axis=0)
        far = exchanged(near, "wide", 1)
        near = after(near, *ready)
        kept, sent = expert(device, near, far, w_gate, w_up, w_down, experts)
        previous.append(sent)
        half = kept + exchanged(sent, "wide", 1).astype(jnp.float32)
        mine, other = half[:masked_row_count], half[masked_row_count:].astype(jnp.bfloat16)
        ready = [other]
        mine = mine + exchanged(other, "wide", 2).astype(jnp.float32)
        if k:
            mine = exchanged(mine.astype(jnp.bfloat16), "wide", 4 * k).astype(jnp.float32)
        total = total + mine
    return total.astype(jnp.bfloat16)


def solution(mesh):
    return jax.shard_map(
        local,
        mesh=mesh,
        in_specs=(
            P(("grp", "wide"), None),
            P(("grp", "wide"), None),
            P(("grp", "wide"), None),
            P(("grp", "wide"), None),
            P(),
            P("grp"),
            P("grp", None),
            P(("grp", "wide"), None),
            P(("grp", "wide"), None),
            P("wide", None, None),
            P("wide", None, None),
            P("wide", None, None),
        ),
        out_specs=P(("grp", "wide"), None),
        check_vma=False,
    )
```

```python
import functools
import math

import jax
import jax.numpy as jnp
from jax import lax
from jax.experimental import pallas as pl
from jax.experimental.pallas import tpu as pltpu
from jax.sharding import PartitionSpec as P


QUERY_HEADS = 32
KEY_VALUE_HEADS = 4
HEAD_SIZE = 64


score_masked_rows = -1e30


def exchanged(shard, axis, distance):
    return lax.ppermute(shard, axis, [(i, i ^ distance) for i in range(lax.axis_size(axis))])


LANES = 128


def cache_kernel(
    device_ref, lengths_ref, positions_ref, own_ref, visit_ref, row_k_ref, row_v_ref, cache_k_ref, cache_v_ref,
    own_out_ref, own_stats_ref, visit_out_ref,
    closed, keys, values, stacked, result, shifts, stats,
):
    group = pl.program_id(0)
    rows = own_ref.shape[0]
    span = cache_k_ref.shape[0]
    pairs = own_ref.shape[1] // LANES
    key_count = keys.shape[0]
    padded = key_count - span
    lane = lax.broadcasted_iota(jnp.int32, (1, LANES), 1)
    low = lane < HEAD_SIZE

    @pl.when(group == 0)
    def _():
        device = device_ref[0]
        start = (device % 2) * span
        length = lengths_ref[device // 2]
        marked = positions_ref[pl.ds(device // 2, 1), :]
        counter = jnp.ones((marked.shape[1], LANES), jnp.bfloat16)
        step = LANES

        def mark(block, carry):
            location = start + block * step + lax.broadcasted_iota(jnp.int32, (step, 1), 0)
            equal = jnp.where(location == marked, 1.0, 0.0).astype(jnp.bfloat16)
            count = jnp.dot(equal, counter, preferred_element_type=jnp.float32)
            shut = ((count > 0.5) | (location >= length)) & (lane == HEAD_SIZE)
            at = pl.ds(pl.multiple_of(block * step, step), step)
            closed[at, :] = jnp.where(shut, score_masked_rows, 0.0).astype(jnp.bfloat16)
            return carry

        lax.fori_loop(0, span // step, mark, 0)
        beyond = lax.broadcasted_iota(jnp.int32, (padded, 1), 0) >= rows
        closed[span:, :] = jnp.where(beyond & (lane == HEAD_SIZE), score_masked_rows, 0.0).astype(jnp.bfloat16)
        stats[...] = jnp.zeros_like(stats)
        if padded > rows:
            keys[span + rows :, :] = closed[span + rows :, :]
            values[span + rows :, :] = jnp.zeros((padded - rows, LANES), jnp.bfloat16)

    first = group % 2 == 0
    zero = jnp.bfloat16(0.0)
    one = jnp.bfloat16(1.0)

    def placed(block, rest):
        wide = block.astype(jnp.float32)
        moved = jnp.where(first, wide, pltpu.roll(wide, HEAD_SIZE, 1)).astype(jnp.bfloat16)
        return jnp.where(low, moved, rest)

    keys[:span, :] = placed(cache_k_ref[...], closed[:span, :])
    values[:span, :] = placed(cache_v_ref[...], one)
    keys[span : span + rows, :] = placed(row_k_ref[...], zero)
    values[span : span + rows, :] = placed(row_v_ref[...], one)
    scale = 1.0 / math.sqrt(HEAD_SIZE)
    marker = jnp.where(lane == HEAD_SIZE, 1.0, 0.0)
    for pair in range(pairs):
        for source, ref in enumerate((own_ref, visit_ref)):
            query = ref[:, pair * LANES : (pair + 1) * LANES].astype(jnp.float32) * scale
            for parity in range(2):
                base = ((parity * pairs + pair) * 2 + source) * rows
                moved = query if parity == 0 else pltpu.roll(query, HEAD_SIZE, 1)
                stacked[base : base + rows, :] = jnp.where(low, moved, marker).astype(jnp.bfloat16)

    chunk = 4 * rows
    for begin in range(0, stacked.shape[0], chunk):
        at = slice(begin, begin + chunk)
        scores = lax.dot_general(
            stacked[at, :], keys[...], (((1,), (1,)), ((), ())), preferred_element_type=jnp.float32
        )
        shift = jnp.max(scores, axis=1, keepdims=True).astype(jnp.bfloat16).astype(jnp.float32)
        weights = jnp.exp(scores - shift).astype(jnp.bfloat16)
        result[at, :] = jnp.dot(weights, values[...], preferred_element_type=jnp.float32)
        shifts[at, :] = jnp.broadcast_to(shift, (chunk, LANES))

    both = 2 * rows
    seen = stats[...]
    for pair in range(pairs):
        even = slice(pair * both, (pair + 1) * both)
        odd = slice((pairs + pair) * both, (pairs + pair + 1) * both)
        joined = jnp.where(low, result[even, :], pltpu.roll(result[odd, :], HEAD_SIZE, 1))
        own_out_ref[:, pair * LANES : (pair + 1) * LANES] = joined[:rows]
        column = pl.multiple_of((group * pairs + pair) * LANES, LANES)
        visit_out_ref[:, pl.ds(column, LANES)] = joined[rows:].astype(jnp.bfloat16)
        for parity, at in enumerate((even, odd)):
            head = (group * pairs + pair) * 2 + parity
            total = result[at, :]
            high = total.astype(jnp.bfloat16).astype(jnp.float32)
            seen = jnp.where(lane == head, shifts[at, :], seen)
            seen = jnp.where(lane == head + 2 * QUERY_HEADS, high, seen)
            seen = jnp.where(lane == head + 3 * QUERY_HEADS, total - high, seen)
    stats[...] = seen

    @pl.when(group == pl.num_programs(0) - 1)
    def _():
        own_stats_ref[...] = stats[:rows].astype(jnp.bfloat16)
        visit_out_ref[:, visit_out_ref.shape[1] - LANES :] = stats[rows:].astype(jnp.bfloat16)


def attend_cache(device, lengths, positions, own, visit, row_key_value, key_value_cache):
    rows, width = own.shape
    span = key_value_cache.shape[0]
    key_count = span + -(-rows // LANES) * LANES
    group_width = width // KEY_VALUE_HEADS
    stack = 2 * rows * (QUERY_HEADS // KEY_VALUE_HEADS)
    half = KEY_VALUE_HEADS * HEAD_SIZE // LANES
    per_block = LANES // HEAD_SIZE
    in_hbm = functools.partial(pltpu.with_memory_space_constraint, memory_space=pltpu.HBM)
    own, row_key_value, key_value_cache, positions = map(in_hbm, (own, row_key_value, key_value_cache, positions))
    return pl.pallas_call(
        cache_kernel,
        grid=(KEY_VALUE_HEADS,),
        in_specs=[
            pl.BlockSpec(memory_space=pltpu.SMEM),
            pl.BlockSpec(memory_space=pltpu.SMEM),
            pl.BlockSpec(positions.shape, lambda g: (0, 0)),
            pl.BlockSpec((rows, group_width), lambda g: (0, g)),
            pl.BlockSpec((rows, group_width), lambda g: (0, g)),
            pl.BlockSpec((rows, LANES), lambda g: (0, g // per_block)),
            pl.BlockSpec((rows, LANES), lambda g: (0, half + g // per_block)),
            pl.BlockSpec((span, LANES), lambda g: (0, g // per_block)),
            pl.BlockSpec((span, LANES), lambda g: (0, half + g // per_block)),
        ],
        out_specs=[
            pl.BlockSpec((rows, group_width), lambda g: (0, g)),
            pl.BlockSpec((rows, LANES), lambda g: (0, 0)),
            pl.BlockSpec((rows, width + LANES), lambda g: (0, 0)),
        ],
        out_shape=[
            jax.ShapeDtypeStruct((rows, width), jnp.float32),
            jax.ShapeDtypeStruct((rows, LANES), jnp.bfloat16),
            jax.ShapeDtypeStruct((rows, width + LANES), jnp.bfloat16),
        ],
        scratch_shapes=[
            pltpu.VMEM((key_count, LANES), jnp.bfloat16),
            pltpu.VMEM((key_count, LANES), jnp.bfloat16),
            pltpu.VMEM((key_count, LANES), jnp.bfloat16),
            pltpu.VMEM((stack, LANES), jnp.bfloat16),
            pltpu.VMEM((stack, LANES), jnp.float32),
            pltpu.VMEM((stack, LANES), jnp.float32),
            pltpu.VMEM((2 * rows, LANES), jnp.float32),
        ],
        compiler_params=pltpu.CompilerParams(vmem_limit_bytes=20 << 20),
        name="cache_attention",
    )(
        device.reshape(1), lengths, positions, own, visit,
        row_key_value, row_key_value, key_value_cache, key_value_cache,
    )


def merge_kernel(own_ref, own_stats_ref, far_ref, resid_ref, gain_ref, shares_ref, payload_ref, residual_ref):
    width = own_ref.shape[1]
    far_stats = far_ref[:, width:]
    head_of = lax.broadcasted_iota(jnp.int32, (LANES, width), 1) // HEAD_SIZE
    stat = lax.broadcasted_iota(jnp.int32, (LANES, width), 0)

    def spread(stats):
        pick_shift = jnp.where(stat == head_of, 1.0, 0.0).astype(jnp.bfloat16)
        pick_total = jnp.where(
            (stat == head_of + 2 * QUERY_HEADS) | (stat == head_of + 3 * QUERY_HEADS), 1.0, 0.0
        ).astype(jnp.bfloat16)
        return (
            jnp.dot(stats, pick_shift, preferred_element_type=jnp.float32),
            jnp.dot(stats, pick_total, preferred_element_type=jnp.float32),
        )

    own_shift, own_total = spread(own_stats_ref[...])
    far_shift, far_total = spread(far_stats)
    joint = jnp.maximum(own_shift, far_shift)
    own_scale = jnp.exp(own_shift - joint)
    far_scale = jnp.exp(far_shift - joint)
    merged = own_ref[...] * own_scale + far_ref[:, :width].astype(jnp.float32) * far_scale
    total = own_total * own_scale + far_total * far_scale
    attn = (merged / total).astype(jnp.bfloat16).astype(jnp.float32)
    residual = resid_ref[...].astype(jnp.float32) + attn
    residual_ref[...] = residual
    power = jnp.mean(residual * residual, axis=1, keepdims=True)
    normed = residual * lax.rsqrt(power + 1e-06) * gain_ref[...]
    payload_ref[:, :width] = normed.astype(jnp.bfloat16)
    payload_ref[:, width:] = shares_ref[...]


def merge(own, own_stats, far, resid, norm_gain, shares):
    rows, width = own.shape
    return pl.pallas_call(
        merge_kernel,
        out_shape=[
            jax.ShapeDtypeStruct((rows, width + shares.shape[1]), jnp.bfloat16),
            jax.ShapeDtypeStruct((rows, width), jnp.float32),
        ],
        compiler_params=pltpu.CompilerParams(vmem_limit_bytes=12 << 20),
        name="merge_norm",
    )(own, own_stats, far, resid, norm_gain.reshape(1, width), shares)


def expert_kernel(device_ref, near_ref, far_ref, gate_ref, up_ref, down_ref, keep_ref, send_ref, *, experts):
    depth = gate_ref.shape[1]
    hidden_width = gate_ref.shape[2]
    rows = jnp.concatenate([near_ref[...], far_ref[...]], axis=0)
    device = device_ref[0]
    column = lax.broadcasted_iota(jnp.int32, (1, rows.shape[1] - depth), 1)
    own_column = (column == device) | (column == device + experts)
    share = jnp.sum(
        jnp.where(own_column, rows[:, depth:].astype(jnp.float32), 0.0), axis=1, keepdims=True
    )
    rows = rows[:, :depth]
    step = 256
    hidden = []
    for begin in range(0, hidden_width, step):
        at = slice(begin, min(begin + step, hidden_width))
        gate_act = jnp.dot(rows, gate_ref[0, :, at], preferred_element_type=jnp.float32)
        up_act = jnp.dot(rows, up_ref[0, :, at], preferred_element_type=jnp.float32)
        hidden.append((jax.nn.silu(gate_act) * up_act).astype(jnp.bfloat16))
    hidden = jnp.concatenate(hidden, axis=1)
    kept = keep_ref.shape[0]
    step = 512
    for begin in range(0, depth, step):
        at = slice(begin, min(begin + step, depth))
        expert_out = jnp.dot(hidden, down_ref[0, :, at], preferred_element_type=jnp.float32)
        partial = share * expert_out.astype(jnp.bfloat16).astype(jnp.float32)
        keep_ref[:, at] = partial[:kept]
        send_ref[:, at] = partial[kept:].astype(jnp.bfloat16)


def expert(device, near, far, w_gate, w_up, w_down, experts):
    rows = near.shape[0]
    depth = w_gate.shape[1]
    return pl.pallas_call(
        functools.partial(expert_kernel, experts=experts),
        in_specs=[pl.BlockSpec(memory_space=pltpu.SMEM)] + [pl.BlockSpec(memory_space=pltpu.VMEM)] * 5,
        out_specs=[pl.BlockSpec(memory_space=pltpu.VMEM)] * 2,
        out_shape=[
            jax.ShapeDtypeStruct((rows, depth), jnp.float32),
            jax.ShapeDtypeStruct((rows, depth), jnp.bfloat16),
        ],
        compiler_params=pltpu.CompilerParams(vmem_limit_bytes=20 << 20),
        name="expert",
    )(device.reshape(1), near, far, w_gate, w_up, w_down)


def local(
    query_rows,
    row_key_value,
    key_value_cache,
    resid,
    norm_gain,
    lengths,
    positions,
    expert_ids,
    gate_scores,
    w_gate,
    w_up,
    w_down,
):
    masked_row_count, _ = resid.shape
    device = lax.axis_index("wide")
    experts = lax.axis_size("wide")
    mix = gate_scores / jnp.sum(gate_scores, axis=-1, keepdims=True)
    shares = jnp.sum(
        jnp.where(expert_ids[..., None] == jnp.arange(experts, dtype=jnp.int32), mix[..., None], 0.0), axis=1
    )
    shares_high = shares.astype(jnp.bfloat16)
    shares_low = (shares - shares_high.astype(jnp.float32)).astype(jnp.bfloat16)
    tail = -(-2 * experts // LANES) * LANES
    filler = jnp.zeros((masked_row_count, tail - 2 * experts), jnp.bfloat16)
    shares = jnp.concatenate([shares_high, shares_low, filler], axis=1)
    visitor = exchanged(query_rows, "wide", 1)
    own, own_stats, hosted = attend_cache(
        device, lengths, positions, query_rows, visitor, row_key_value, key_value_cache
    )
    far = exchanged(hosted, "wide", 1)
    payload, residual = merge(own, own_stats, far, resid, norm_gain, shares)
    planes = experts // 4
    blocks = [payload]
    total = residual
    beside, near, far = [], [None] * planes, [None] * planes
    for k in range(1, planes):
        low_bit = k & -k
        blocks.append(exchanged(blocks[k - low_bit], "wide", 4 * low_bit))
    for k in range(planes):
        low_bit = k & -k
        if k > low_bit:
            beside.append(exchanged(beside[k - low_bit], "wide", 4 * low_bit))
        else:
            beside.append(exchanged(blocks[k], "wide", 2))
        near[k] = jnp.concatenate([blocks[k], beside[k]], axis=0)
        far[k] = exchanged(near[k], "wide", 1)
    for k in range(planes):
        kept, sent = expert(device, near[k], far[k], w_gate, w_up, w_down, experts)
        sent = exchanged(sent, "wide", 1)
        half = kept + sent.astype(jnp.float32)
        mine, other = half[:masked_row_count], half[masked_row_count:].astype(jnp.bfloat16)
        other = exchanged(other, "wide", 2)
        mine = mine + other.astype(jnp.float32)
        if k:
            mine = exchanged(mine.astype(jnp.bfloat16), "wide", 4 * k).astype(jnp.float32)
        total = total + mine
    return total.astype(jnp.bfloat16)


def solution(mesh):
    return jax.shard_map(
        local,
        mesh=mesh,
        in_specs=(
            P(("grp", "wide"), None),
            P(("grp", "wide"), None),
            P(("grp", "wide"), None),
            P(("grp", "wide"), None),
            P(),
            P("grp"),
            P("grp", None),
            P(("grp", "wide"), None),
            P(("grp", "wide"), None),
            P("wide", None, None),
            P("wide", None, None),
            P("wide", None, None),
        ),
        out_specs=P(("grp", "wide"), None),
        check_vma=False,
    )
```

```python
import functools
import math

import jax
import jax.numpy as jnp
from jax import lax
from jax.experimental import pallas as pl
from jax.experimental.pallas import tpu as pltpu
from jax.sharding import PartitionSpec as P


QUERY_HEADS = 32
KEY_VALUE_HEADS = 4
HEAD_SIZE = 64


score_masked_rows = -1e30


def exchanged(shard, axis, distance):
    return lax.ppermute(shard, axis, [(i, i ^ distance) for i in range(lax.axis_size(axis))])


LANES = 128


def cache_kernel(
    device_ref, lengths_ref, positions_ref, own_ref, visit_ref, row_k_ref, row_v_ref, cache_k_ref, cache_v_ref,
    own_out_ref, own_stats_ref, visit_out_ref,
    keys, values, stacked, buffer, weights, result, shifts, stats,
):
    group = pl.program_id(0)
    rows = own_ref.shape[0]
    span = cache_k_ref.shape[0]
    pairs = own_ref.shape[1] // LANES
    key_count = keys.shape[0]
    padded = key_count - span
    lane = lax.broadcasted_iota(jnp.int32, (1, LANES), 1)
    low = lane < HEAD_SIZE

    @pl.when(group == 0)
    def _():
        device = device_ref[0]
        start = (device % 2) * span
        length = lengths_ref[device // 2]
        marked = positions_ref[pl.ds(device // 2, 1), :]
        counter = jnp.ones((marked.shape[1], LANES), jnp.bfloat16)
        step = LANES

        def mark(block, carry):
            location = start + block * step + lax.broadcasted_iota(jnp.int32, (step, 1), 0)
            equal = jnp.where(location == marked, 1.0, 0.0).astype(jnp.bfloat16)
            count = jnp.dot(equal, counter, preferred_element_type=jnp.float32)
            shut = ((count > 0.5) | (location >= length)) & (lane == 0)
            at = pl.ds(pl.multiple_of(block * step, step), step)
            keys[at, LANES:] = jnp.where(shut, score_masked_rows, 0.0).astype(jnp.bfloat16)
            return carry

        lax.fori_loop(0, span // step, mark, 0)
        beyond = lax.broadcasted_iota(jnp.int32, (padded, 1), 0) >= rows
        keys[span:, LANES:] = jnp.where(beyond & (lane == 0), score_masked_rows, 0.0).astype(jnp.bfloat16)
        values[:, LANES:] = jnp.ones((key_count, LANES), jnp.bfloat16)
        stacked[:, LANES:] = jnp.where(
            lax.broadcasted_iota(jnp.int32, (stacked.shape[0], LANES), 1) == 0, 1.0, 0.0
        ).astype(jnp.bfloat16)
        stats[...] = jnp.zeros_like(stats)
        if padded > rows:
            keys[span + rows :, :LANES] = jnp.zeros((padded - rows, LANES), jnp.bfloat16)
            values[span + rows :, :LANES] = jnp.zeros((padded - rows, LANES), jnp.bfloat16)

    @pl.when(group % 2 == 0)
    def _():
        keys[:span, :LANES] = cache_k_ref[...]
        values[:span, :LANES] = cache_v_ref[...]
        keys[span : span + rows, :LANES] = row_k_ref[...]
        values[span : span + rows, :LANES] = row_v_ref[...]

    first = group % 2 == 0
    side = low == first
    scale = 1.0 / math.sqrt(HEAD_SIZE)
    for pair in range(pairs):
        for source, ref in enumerate((own_ref, visit_ref)):
            query = ref[:, pair * LANES : (pair + 1) * LANES].astype(jnp.float32) * scale
            turned = pltpu.roll(query, HEAD_SIZE, 1)
            for parity in range(2):
                base = ((parity * pairs + pair) * 2 + source) * rows
                moved = jnp.where(first == (parity == 0), query, turned)
                stacked[base : base + rows, :LANES] = jnp.where(side, moved, 0.0).astype(jnp.bfloat16)

    chunk = buffer.shape[1]
    wide = 2 * LANES

    def score(turn):
        query = stacked[turn * chunk : (turn + 1) * chunk, :]
        highest = None
        for begin in range(0, key_count, wide):
            end = min(begin + wide, key_count)
            tile = lax.dot_general(
                query, keys[begin:end, :], (((1,), (1,)), ((), ())), preferred_element_type=jnp.float32
            )
            buffer[turn % 2, :, begin:end] = tile
            for lanes in range(0, end - begin, LANES):
                part = tile[:, lanes : lanes + LANES]
                highest = part if highest is None else jnp.maximum(highest, part)
        return jnp.max(highest, axis=1, keepdims=True).astype(jnp.bfloat16).astype(jnp.float32)

    def weigh(turn, shift):
        at = slice(turn * chunk, (turn + 1) * chunk)
        shifts[at, :] = jnp.broadcast_to(shift, (chunk, LANES))
        for begin in range(0, key_count, wide):
            end = min(begin + wide, key_count)
            weights[turn % 2, :, begin:end] = jnp.exp(buffer[turn % 2, :, begin:end] - shift).astype(jnp.bfloat16)
        result[at, :] = jnp.dot(weights[turn % 2], values[...], preferred_element_type=jnp.float32)

    turns = stacked.shape[0] // chunk
    shift = score(0)
    for turn in range(turns):
        ahead = score(turn + 1) if turn + 1 < turns else None
        weigh(turn, shift)
        shift = ahead

    both = 2 * rows
    seen = stats[...]
    for pair in range(pairs):
        even = slice(pair * both, (pair + 1) * both)
        odd = slice((pairs + pair) * both, (pairs + pair + 1) * both)
        left, right = result[even, :LANES], result[odd, :LANES]
        left = jnp.where(first, left, pltpu.roll(left, HEAD_SIZE, 1))
        right = jnp.where(first, pltpu.roll(right, HEAD_SIZE, 1), right)
        joined = jnp.where(low, left, right)
        own_out_ref[:, pair * LANES : (pair + 1) * LANES] = joined[:rows]
        column = pl.multiple_of((group * pairs + pair) * LANES, LANES)
        visit_out_ref[:, pl.ds(column, LANES)] = joined[rows:].astype(jnp.bfloat16)
        for parity, at in enumerate((even, odd)):
            head = (group * pairs + pair) * 2 + parity
            total = result[at, LANES:]
            high = total.astype(jnp.bfloat16).astype(jnp.float32)
            seen = jnp.where(lane == head, shifts[at, :], seen)
            seen = jnp.where(lane == head + 2 * QUERY_HEADS, high, seen)
            seen = jnp.where(lane == head + 3 * QUERY_HEADS, total - high, seen)
    stats[...] = seen

    @pl.when(group == pl.num_programs(0) - 1)
    def _():
        own_stats_ref[...] = stats[:rows].astype(jnp.bfloat16)
        visit_out_ref[:, visit_out_ref.shape[1] - LANES :] = stats[rows:].astype(jnp.bfloat16)


def attend_cache(device, lengths, positions, own, visit, row_key_value, key_value_cache):
    rows, width = own.shape
    span = key_value_cache.shape[0]
    key_count = span + -(-rows // LANES) * LANES
    group_width = width // KEY_VALUE_HEADS
    stack = 2 * rows * (QUERY_HEADS // KEY_VALUE_HEADS)
    half = KEY_VALUE_HEADS * HEAD_SIZE // LANES
    per_block = LANES // HEAD_SIZE
    in_hbm = functools.partial(pltpu.with_memory_space_constraint, memory_space=pltpu.HBM)
    own, row_key_value, key_value_cache = map(in_hbm, (own, row_key_value, key_value_cache))
    lengths, positions = in_hbm(lengths), in_hbm(positions)
    return pl.pallas_call(
        cache_kernel,
        grid=(KEY_VALUE_HEADS,),
        in_specs=[
            pl.BlockSpec(memory_space=pltpu.SMEM),
            pl.BlockSpec(memory_space=pltpu.SMEM),
            pl.BlockSpec(positions.shape, lambda g: (0, 0)),
            pl.BlockSpec((rows, group_width), lambda g: (0, g)),
            pl.BlockSpec((rows, group_width), lambda g: (0, g)),
            pl.BlockSpec((rows, LANES), lambda g: (0, g // per_block)),
            pl.BlockSpec((rows, LANES), lambda g: (0, half + g // per_block)),
            pl.BlockSpec((span, LANES), lambda g: (0, g // per_block)),
            pl.BlockSpec((span, LANES), lambda g: (0, half + g // per_block)),
        ],
        out_specs=[
            pl.BlockSpec((rows, group_width), lambda g: (0, g)),
            pl.BlockSpec((rows, LANES), lambda g: (0, 0)),
            pl.BlockSpec((rows, width + LANES), lambda g: (0, 0)),
        ],
        out_shape=[
            jax.ShapeDtypeStruct((rows, width), jnp.float32),
            jax.ShapeDtypeStruct((rows, LANES), jnp.bfloat16),
            jax.ShapeDtypeStruct((rows, width + LANES), jnp.bfloat16),
        ],
        scratch_shapes=[
            pltpu.VMEM((key_count, 2 * LANES), jnp.bfloat16),
            pltpu.VMEM((key_count, 2 * LANES), jnp.bfloat16),
            pltpu.VMEM((stack, 2 * LANES), jnp.bfloat16),
            pltpu.VMEM((2, 4 * rows, key_count), jnp.float32),
            pltpu.VMEM((2, 4 * rows, key_count), jnp.bfloat16),
            pltpu.VMEM((stack, 2 * LANES), jnp.float32),
            pltpu.VMEM((stack, LANES), jnp.float32),
            pltpu.VMEM((2 * rows, LANES), jnp.float32),
        ],
        compiler_params=pltpu.CompilerParams(vmem_limit_bytes=20 << 20),
        name="cache_attention",
    )(
        device.reshape(1), lengths, positions, own, visit,
        row_key_value, row_key_value, key_value_cache, key_value_cache,
    )


def merge_kernel(own_ref, own_stats_ref, far_ref, resid_ref, gain_ref, shares_ref, payload_ref, residual_ref):
    width = own_ref.shape[1]
    far_stats = far_ref[:, width:]
    head_of = lax.broadcasted_iota(jnp.int32, (LANES, width), 1) // HEAD_SIZE
    stat = lax.broadcasted_iota(jnp.int32, (LANES, width), 0)

    def spread(stats):
        pick_shift = jnp.where(stat == head_of, 1.0, 0.0).astype(jnp.bfloat16)
        pick_total = jnp.where(
            (stat == head_of + 2 * QUERY_HEADS) | (stat == head_of + 3 * QUERY_HEADS), 1.0, 0.0
        ).astype(jnp.bfloat16)
        return (
            jnp.dot(stats, pick_shift, preferred_element_type=jnp.float32),
            jnp.dot(stats, pick_total, preferred_element_type=jnp.float32),
        )

    own_shift, own_total = spread(own_stats_ref[...])
    far_shift, far_total = spread(far_stats)
    joint = jnp.maximum(own_shift, far_shift)
    own_scale = jnp.exp(own_shift - joint)
    far_scale = jnp.exp(far_shift - joint)
    merged = own_ref[...] * own_scale + far_ref[:, :width].astype(jnp.float32) * far_scale
    total = own_total * own_scale + far_total * far_scale
    attn = (merged / total).astype(jnp.bfloat16).astype(jnp.float32)
    residual = resid_ref[...].astype(jnp.float32) + attn
    residual_ref[...] = residual
    power = jnp.mean(residual * residual, axis=1, keepdims=True)
    normed = residual * lax.rsqrt(power + 1e-06) * gain_ref[...]
    payload_ref[:, :width] = normed.astype(jnp.bfloat16)
    payload_ref[:, width:] = shares_ref[...]


def merge(own, own_stats, far, resid, norm_gain, shares):
    rows, width = own.shape
    return pl.pallas_call(
        merge_kernel,
        out_shape=[
            jax.ShapeDtypeStruct((rows, width + shares.shape[1]), jnp.bfloat16),
            jax.ShapeDtypeStruct((rows, width), jnp.float32),
        ],
        compiler_params=pltpu.CompilerParams(vmem_limit_bytes=12 << 20),
        name="merge_norm",
    )(own, own_stats, far, resid, norm_gain.reshape(1, width), shares)


def expert_kernel(device_ref, near_ref, far_ref, gate_ref, up_ref, down_ref, keep_ref, send_ref, *, experts):
    depth = gate_ref.shape[1]
    hidden_width = gate_ref.shape[2]
    rows = jnp.concatenate([near_ref[...], far_ref[...]], axis=0)
    device = device_ref[0]
    column = lax.broadcasted_iota(jnp.int32, (1, rows.shape[1] - depth), 1)
    own_column = (column == device) | (column == device + experts)
    share = jnp.sum(
        jnp.where(own_column, rows[:, depth:].astype(jnp.float32), 0.0), axis=1, keepdims=True
    )
    rows = rows[:, :depth]
    step = 256
    hidden = []
    for begin in range(0, hidden_width, step):
        at = slice(begin, min(begin + step, hidden_width))
        gate_act = jnp.dot(rows, gate_ref[0, :, at], preferred_element_type=jnp.float32)
        up_act = jnp.dot(rows, up_ref[0, :, at], preferred_element_type=jnp.float32)
        hidden.append((jax.nn.silu(gate_act) * up_act).astype(jnp.bfloat16))
    hidden = jnp.concatenate(hidden, axis=1)
    kept = keep_ref.shape[0]
    step = 512
    for begin in range(0, depth, step):
        at = slice(begin, min(begin + step, depth))
        expert_out = jnp.dot(hidden, down_ref[0, :, at], preferred_element_type=jnp.float32)
        partial = share * expert_out.astype(jnp.bfloat16).astype(jnp.float32)
        keep_ref[:, at] = partial[:kept]
        send_ref[:, at] = partial[kept:].astype(jnp.bfloat16)


def expert(device, near, far, w_gate, w_up, w_down, experts):
    rows = near.shape[0]
    depth = w_gate.shape[1]
    return pl.pallas_call(
        functools.partial(expert_kernel, experts=experts),
        in_specs=[pl.BlockSpec(memory_space=pltpu.SMEM)] + [pl.BlockSpec(memory_space=pltpu.VMEM)] * 5,
        out_specs=[pl.BlockSpec(memory_space=pltpu.VMEM)] * 2,
        out_shape=[
            jax.ShapeDtypeStruct((rows, depth), jnp.float32),
            jax.ShapeDtypeStruct((rows, depth), jnp.bfloat16),
        ],
        compiler_params=pltpu.CompilerParams(vmem_limit_bytes=20 << 20),
        name="expert",
    )(device.reshape(1), near, far, w_gate, w_up, w_down)


def local(
    query_rows,
    row_key_value,
    key_value_cache,
    resid,
    norm_gain,
    lengths,
    positions,
    expert_ids,
    gate_scores,
    w_gate,
    w_up,
    w_down,
):
    masked_row_count, _ = resid.shape
    device = lax.axis_index("wide")
    experts = lax.axis_size("wide")
    mix = gate_scores / jnp.sum(gate_scores, axis=-1, keepdims=True)
    shares = jnp.sum(
        jnp.where(expert_ids[..., None] == jnp.arange(experts, dtype=jnp.int32), mix[..., None], 0.0), axis=1
    )
    shares_high = shares.astype(jnp.bfloat16)
    shares_low = (shares - shares_high.astype(jnp.float32)).astype(jnp.bfloat16)
    tail = -(-2 * experts // LANES) * LANES
    filler = jnp.zeros((masked_row_count, tail - 2 * experts), jnp.bfloat16)
    shares = jnp.concatenate([shares_high, shares_low, filler], axis=1)
    visitor = exchanged(query_rows, "wide", 1)
    own, own_stats, hosted = attend_cache(
        device, lengths, positions, query_rows, visitor, row_key_value, key_value_cache
    )
    far = exchanged(hosted, "wide", 1)
    payload, residual = merge(own, own_stats, far, resid, norm_gain, shares)
    planes = experts // 4
    blocks = [payload]
    total = residual
    beside, near, far = [], [None] * planes, [None] * planes
    for k in range(1, planes):
        low_bit = k & -k
        blocks.append(exchanged(blocks[k - low_bit], "wide", 4 * low_bit))
    for k in range(planes):
        low_bit = k & -k
        if k > low_bit:
            beside.append(exchanged(beside[k - low_bit], "wide", 4 * low_bit))
        else:
            beside.append(exchanged(blocks[k], "wide", 2))
        near[k] = jnp.concatenate([blocks[k], beside[k]], axis=0)
        far[k] = exchanged(near[k], "wide", 1)
    for k in range(planes):
        kept, sent = expert(device, near[k], far[k], w_gate, w_up, w_down, experts)
        sent = exchanged(sent, "wide", 1)
        half = kept + sent.astype(jnp.float32)
        mine, other = half[:masked_row_count], half[masked_row_count:].astype(jnp.bfloat16)
        other = exchanged(other, "wide", 2)
        mine = mine + other.astype(jnp.float32)
        if k:
            mine = exchanged(mine.astype(jnp.bfloat16), "wide", 4 * k).astype(jnp.float32)
        total = total + mine
    return total.astype(jnp.bfloat16)


def solution(mesh):
    return jax.shard_map(
        local,
        mesh=mesh,
        in_specs=(
            P(("grp", "wide"), None),
            P(("grp", "wide"), None),
            P(("grp", "wide"), None),
            P(("grp", "wide"), None),
            P(),
            P("grp"),
            P("grp", None),
            P(("grp", "wide"), None),
            P(("grp", "wide"), None),
            P("wide", None, None),
            P("wide", None, None),
            P("wide", None, None),
        ),
        out_specs=P(("grp", "wide"), None),
        check_vma=False,
    )
```

```python
import functools
import math

import jax
import jax.numpy as jnp
from jax import lax
from jax.experimental import pallas as pl
from jax.experimental.pallas import tpu as pltpu
from jax.sharding import PartitionSpec as P


QUERY_HEADS = 32
KEY_VALUE_HEADS = 4
HEAD_SIZE = 64


score_masked_rows = -1e30


def exchanged(shard, axis, distance):
    return lax.ppermute(shard, axis, [(i, i ^ distance) for i in range(lax.axis_size(axis))])


LANES = 128


def cache_kernel(
    device_ref, lengths_ref, positions_ref, own_ref, visit_ref, row_k_ref, row_v_ref, cache_k_ref, cache_v_ref,
    own_out_ref, own_stats_ref, visit_out_ref,
    keys, values, stacked, buffer, weights, result, shifts, stats,
):
    group = pl.program_id(0)
    rows = own_ref.shape[0]
    span = cache_k_ref.shape[0]
    pairs = own_ref.shape[1] // LANES
    key_count = keys.shape[0]
    padded = key_count - span
    lane = lax.broadcasted_iota(jnp.int32, (1, LANES), 1)
    low = lane < HEAD_SIZE

    @pl.when(group == 0)
    def _():
        device = device_ref[0]
        start = (device % 2) * span
        length = lengths_ref[device // 2]
        marked = positions_ref[pl.ds(device // 2, 1), :]
        counter = jnp.ones((marked.shape[1], LANES), jnp.bfloat16)
        step = LANES

        def mark(block, carry):
            location = start + block * step + lax.broadcasted_iota(jnp.int32, (step, 1), 0)
            equal = jnp.where(location == marked, 1.0, 0.0).astype(jnp.bfloat16)
            count = jnp.dot(equal, counter, preferred_element_type=jnp.float32)
            shut = ((count > 0.5) | (location >= length)) & (lane == 0)
            at = pl.ds(pl.multiple_of(block * step, step), step)
            keys[at, LANES:] = jnp.where(shut, score_masked_rows, 0.0).astype(jnp.bfloat16)
            return carry

        lax.fori_loop(0, span // step, mark, 0)
        beyond = lax.broadcasted_iota(jnp.int32, (padded, 1), 0) >= rows
        keys[span:, LANES:] = jnp.where(beyond & (lane == 0), score_masked_rows, 0.0).astype(jnp.bfloat16)
        values[:, LANES:] = jnp.ones((key_count, LANES), jnp.bfloat16)
        stacked[:, LANES:] = jnp.where(
            lax.broadcasted_iota(jnp.int32, (stacked.shape[0], LANES), 1) == 0, 1.0, 0.0
        ).astype(jnp.bfloat16)
        stats[...] = jnp.zeros_like(stats)
        if padded > rows:
            keys[span + rows :, :LANES] = jnp.zeros((padded - rows, LANES), jnp.bfloat16)
            values[span + rows :, :LANES] = jnp.zeros((padded - rows, LANES), jnp.bfloat16)

    @pl.when(group % 2 == 0)
    def _():
        keys[:span, :LANES] = cache_k_ref[...]
        values[:span, :LANES] = cache_v_ref[...]
        keys[span : span + rows, :LANES] = row_k_ref[...]
        values[span : span + rows, :LANES] = row_v_ref[...]

    first = group % 2 == 0
    side = low == first
    scale = 1.0 / math.sqrt(HEAD_SIZE)
    for pair in range(pairs):
        for source, ref in enumerate((own_ref, visit_ref)):
            query = ref[:, pair * LANES : (pair + 1) * LANES].astype(jnp.float32) * scale
            turned = pltpu.roll(query, HEAD_SIZE, 1)
            for parity in range(2):
                base = ((parity * pairs + pair) * 2 + source) * rows
                moved = jnp.where(first == (parity == 0), query, turned)
                stacked[base : base + rows, :LANES] = jnp.where(side, moved, 0.0).astype(jnp.bfloat16)

    chunk = buffer.shape[1]
    wide = 2 * LANES

    def score(turn):
        query = stacked[turn * chunk : (turn + 1) * chunk, :]
        highest = None
        for begin in range(0, key_count, wide):
            end = min(begin + wide, key_count)
            tile = lax.dot_general(
                query, keys[begin:end, :], (((1,), (1,)), ((), ())), preferred_element_type=jnp.float32
            )
            buffer[turn % 2, :, begin:end] = tile
            for lanes in range(0, end - begin, LANES):
                part = tile[:, lanes : lanes + LANES]
                highest = part if highest is None else jnp.maximum(highest, part)
        return jnp.max(highest, axis=1, keepdims=True).astype(jnp.bfloat16).astype(jnp.float32)

    def weigh(turn, shift):
        at = slice(turn * chunk, (turn + 1) * chunk)
        shifts[at, :] = jnp.broadcast_to(shift, (chunk, LANES))
        for begin in range(0, key_count, wide):
            end = min(begin + wide, key_count)
            weights[turn % 2, :, begin:end] = jnp.exp(buffer[turn % 2, :, begin:end] - shift).astype(jnp.bfloat16)
        result[at, :] = jnp.dot(weights[turn % 2], values[...], preferred_element_type=jnp.float32)

    turns = stacked.shape[0] // chunk
    shift = score(0)
    for turn in range(turns):
        ahead = score(turn + 1) if turn + 1 < turns else None
        weigh(turn, shift)
        shift = ahead

    both = 2 * rows
    seen = stats[...]
    for pair in range(pairs):
        even = slice(pair * both, (pair + 1) * both)
        odd = slice((pairs + pair) * both, (pairs + pair + 1) * both)
        left, right = result[even, :LANES], result[odd, :LANES]
        left = jnp.where(first, left, pltpu.roll(left, HEAD_SIZE, 1))
        right = jnp.where(first, pltpu.roll(right, HEAD_SIZE, 1), right)
        joined = jnp.where(low, left, right)
        own_out_ref[:, pair * LANES : (pair + 1) * LANES] = joined[:rows]
        column = pl.multiple_of((group * pairs + pair) * LANES, LANES)
        visit_out_ref[:, pl.ds(column, LANES)] = joined[rows:].astype(jnp.bfloat16)
        for parity, at in enumerate((even, odd)):
            head = (group * pairs + pair) * 2 + parity
            total = result[at, LANES:]
            high = total.astype(jnp.bfloat16).astype(jnp.float32)
            seen = jnp.where(lane == head, shifts[at, :], seen)
            seen = jnp.where(lane == head + 2 * QUERY_HEADS, high, seen)
            seen = jnp.where(lane == head + 3 * QUERY_HEADS, total - high, seen)
    stats[...] = seen

    @pl.when(group == pl.num_programs(0) - 1)
    def _():
        own_stats_ref[...] = stats[:rows].astype(jnp.bfloat16)
        visit_out_ref[:, visit_out_ref.shape[1] - LANES :] = stats[rows:].astype(jnp.bfloat16)


def attend_cache(device, lengths, positions, own, visit, row_key_value, key_value_cache):
    rows, width = own.shape
    span = key_value_cache.shape[0]
    key_count = span + -(-rows // LANES) * LANES
    group_width = width // KEY_VALUE_HEADS
    stack = 2 * rows * (QUERY_HEADS // KEY_VALUE_HEADS)
    half = KEY_VALUE_HEADS * HEAD_SIZE // LANES
    per_block = LANES // HEAD_SIZE
    in_hbm = functools.partial(pltpu.with_memory_space_constraint, memory_space=pltpu.HBM)
    own, row_key_value, key_value_cache = map(in_hbm, (own, row_key_value, key_value_cache))
    lengths, positions = in_hbm(lengths), in_hbm(positions)
    return pl.pallas_call(
        cache_kernel,
        grid=(KEY_VALUE_HEADS,),
        in_specs=[
            pl.BlockSpec(memory_space=pltpu.SMEM),
            pl.BlockSpec(memory_space=pltpu.SMEM),
            pl.BlockSpec(positions.shape, lambda g: (0, 0)),
            pl.BlockSpec((rows, group_width), lambda g: (0, g)),
            pl.BlockSpec((rows, group_width), lambda g: (0, g)),
            pl.BlockSpec((rows, LANES), lambda g: (0, g // per_block)),
            pl.BlockSpec((rows, LANES), lambda g: (0, half + g // per_block)),
            pl.BlockSpec((span, LANES), lambda g: (0, g // per_block)),
            pl.BlockSpec((span, LANES), lambda g: (0, half + g // per_block)),
        ],
        out_specs=[
            pl.BlockSpec((rows, group_width), lambda g: (0, g)),
            pl.BlockSpec((rows, LANES), lambda g: (0, 0)),
            pl.BlockSpec((rows, width + LANES), lambda g: (0, 0)),
        ],
        out_shape=[
            jax.ShapeDtypeStruct((rows, width), jnp.float32),
            jax.ShapeDtypeStruct((rows, LANES), jnp.bfloat16),
            jax.ShapeDtypeStruct((rows, width + LANES), jnp.bfloat16),
        ],
        scratch_shapes=[
            pltpu.VMEM((key_count, 2 * LANES), jnp.bfloat16),
            pltpu.VMEM((key_count, 2 * LANES), jnp.bfloat16),
            pltpu.VMEM((stack, 2 * LANES), jnp.bfloat16),
            pltpu.VMEM((2, 4 * rows, key_count), jnp.float32),
            pltpu.VMEM((2, 4 * rows, key_count), jnp.bfloat16),
            pltpu.VMEM((stack, 2 * LANES), jnp.float32),
            pltpu.VMEM((stack, LANES), jnp.float32),
            pltpu.VMEM((2 * rows, LANES), jnp.float32),
        ],
        compiler_params=pltpu.CompilerParams(vmem_limit_bytes=20 << 20),
        name="cache_attention",
    )(
        device.reshape(1), lengths, positions, own, visit,
        row_key_value, row_key_value, key_value_cache, key_value_cache,
    )


def merge_kernel(own_ref, own_stats_ref, far_ref, resid_ref, gain_ref, shares_ref, payload_ref, residual_ref):
    width = own_ref.shape[1]
    far_stats = far_ref[:, width:]
    head_of = lax.broadcasted_iota(jnp.int32, (LANES, width), 1) // HEAD_SIZE
    stat = lax.broadcasted_iota(jnp.int32, (LANES, width), 0)

    def spread(stats):
        pick_shift = jnp.where(stat == head_of, 1.0, 0.0).astype(jnp.bfloat16)
        pick_total = jnp.where(
            (stat == head_of + 2 * QUERY_HEADS) | (stat == head_of + 3 * QUERY_HEADS), 1.0, 0.0
        ).astype(jnp.bfloat16)
        return (
            jnp.dot(stats, pick_shift, preferred_element_type=jnp.float32),
            jnp.dot(stats, pick_total, preferred_element_type=jnp.float32),
        )

    own_shift, own_total = spread(own_stats_ref[...])
    far_shift, far_total = spread(far_stats)
    joint = jnp.maximum(own_shift, far_shift)
    own_scale = jnp.exp(own_shift - joint)
    far_scale = jnp.exp(far_shift - joint)
    merged = own_ref[...] * own_scale + far_ref[:, :width].astype(jnp.float32) * far_scale
    total = own_total * own_scale + far_total * far_scale
    attn = (merged / total).astype(jnp.bfloat16).astype(jnp.float32)
    residual = resid_ref[...].astype(jnp.float32) + attn
    residual_ref[...] = residual
    power = jnp.mean(residual * residual, axis=1, keepdims=True)
    normed = residual * lax.rsqrt(power + 1e-06) * gain_ref[...]
    payload_ref[:, :width] = normed.astype(jnp.bfloat16)
    payload_ref[:, width:] = shares_ref[...]


def merge(own, own_stats, far, resid, norm_gain, shares):
    rows, width = own.shape
    return pl.pallas_call(
        merge_kernel,
        out_shape=[
            jax.ShapeDtypeStruct((rows, width + shares.shape[1]), jnp.bfloat16),
            jax.ShapeDtypeStruct((rows, width), jnp.float32),
        ],
        compiler_params=pltpu.CompilerParams(vmem_limit_bytes=12 << 20),
        name="merge_norm",
    )(own, own_stats, far, resid, norm_gain.reshape(1, width), shares)


def expert_kernel(device_ref, near_ref, far_ref, gate_ref, up_ref, down_ref, keep_ref, send_ref, *, experts):
    depth = gate_ref.shape[1]
    hidden_width = gate_ref.shape[2]
    rows = jnp.concatenate([near_ref[...], far_ref[...]], axis=0)
    device = device_ref[0]
    column = lax.broadcasted_iota(jnp.int32, (1, rows.shape[1] - depth), 1)
    own_column = (column == device) | (column == device + experts)
    share = jnp.sum(
        jnp.where(own_column, rows[:, depth:].astype(jnp.float32), 0.0), axis=1, keepdims=True
    )
    rows = rows[:, :depth]
    step = 256
    hidden = []
    for begin in range(0, hidden_width, step):
        at = slice(begin, min(begin + step, hidden_width))
        gate_act = jnp.dot(rows, gate_ref[0, :, at], preferred_element_type=jnp.float32)
        up_act = jnp.dot(rows, up_ref[0, :, at], preferred_element_type=jnp.float32)
        hidden.append((jax.nn.silu(gate_act) * up_act).astype(jnp.bfloat16))
    hidden = jnp.concatenate(hidden, axis=1)
    kept = keep_ref.shape[0]
    step = 512
    for begin in range(0, depth, step):
        at = slice(begin, min(begin + step, depth))
        expert_out = jnp.dot(hidden, down_ref[0, :, at], preferred_element_type=jnp.float32)
        partial = share * expert_out.astype(jnp.bfloat16).astype(jnp.float32)
        keep_ref[:, at] = partial[:kept]
        send_ref[:, at] = partial[kept:].astype(jnp.bfloat16)


def expert(device, near, far, w_gate, w_up, w_down, experts):
    rows = near.shape[0]
    depth = w_gate.shape[1]
    return pl.pallas_call(
        functools.partial(expert_kernel, experts=experts),
        in_specs=[pl.BlockSpec(memory_space=pltpu.SMEM)] + [pl.BlockSpec(memory_space=pltpu.VMEM)] * 5,
        out_specs=[pl.BlockSpec(memory_space=pltpu.VMEM)] * 2,
        out_shape=[
            jax.ShapeDtypeStruct((rows, depth), jnp.float32),
            jax.ShapeDtypeStruct((rows, depth), jnp.bfloat16),
        ],
        compiler_params=pltpu.CompilerParams(vmem_limit_bytes=20 << 20),
        name="expert",
    )(device.reshape(1), near, far, w_gate, w_up, w_down)


def local(
    query_rows,
    row_key_value,
    key_value_cache,
    resid,
    norm_gain,
    lengths,
    positions,
    expert_ids,
    gate_scores,
    w_gate,
    w_up,
    w_down,
):
    masked_row_count, _ = resid.shape
    device = lax.axis_index("wide")
    experts = lax.axis_size("wide")
    mix = gate_scores / jnp.sum(gate_scores, axis=-1, keepdims=True)
    shares = jnp.sum(
        jnp.where(expert_ids[..., None] == jnp.arange(experts, dtype=jnp.int32), mix[..., None], 0.0), axis=1
    )
    shares_high = shares.astype(jnp.bfloat16)
    shares_low = (shares - shares_high.astype(jnp.float32)).astype(jnp.bfloat16)
    tail = -(-2 * experts // LANES) * LANES
    filler = jnp.zeros((masked_row_count, tail - 2 * experts), jnp.bfloat16)
    shares = jnp.concatenate([shares_high, shares_low, filler], axis=1)
    visitor = exchanged(query_rows, "wide", 1)
    own, own_stats, hosted = attend_cache(
        device, lengths, positions, query_rows, visitor, row_key_value, key_value_cache
    )
    far = exchanged(hosted, "wide", 1)
    payload, residual = merge(own, own_stats, far, resid, norm_gain, shares)
    planes = experts // 4
    blocks = [payload]
    total = residual
    beside, near, far = [], [None] * planes, [None] * planes
    for k in range(1, planes):
        low_bit = k & -k
        blocks.append(exchanged(blocks[k - low_bit], "wide", 4 * low_bit))
    for k in range(planes):
        low_bit = k & -k
        if k > low_bit:
            beside.append(exchanged(beside[k - low_bit], "wide", 4 * low_bit))
        else:
            beside.append(exchanged(blocks[k], "wide", 2))
        near[k] = jnp.concatenate([blocks[k], beside[k]], axis=0)
        far[k] = exchanged(near[k], "wide", 1)
    for k in range(planes):
        kept, sent = expert(device, near[k], far[k], w_gate, w_up, w_down, experts)
        sent = exchanged(sent, "wide", 1)
        half = kept + sent.astype(jnp.float32)
        mine, other = half[:masked_row_count], half[masked_row_count:].astype(jnp.bfloat16)
        other = exchanged(other, "wide", 2)
        mine = mine + other.astype(jnp.float32)
        if k % 2 == 0 and k:
            relayed = exchanged(mine.astype(jnp.bfloat16), "wide", 4).astype(jnp.float32)
            continue
        if k > 1:
            mine = mine + relayed
        if k:
            mine = exchanged(mine.astype(jnp.bfloat16), "wide", 4 * k).astype(jnp.float32)
        total = total + mine
    return total.astype(jnp.bfloat16)


def solution(mesh):
    return jax.shard_map(
        local,
        mesh=mesh,
        in_specs=(
            P(("grp", "wide"), None),
            P(("grp", "wide"), None),
            P(("grp", "wide"), None),
            P(("grp", "wide"), None),
            P(),
            P("grp"),
            P("grp", None),
            P(("grp", "wide"), None),
            P(("grp", "wide"), None),
            P("wide", None, None),
            P("wide", None, None),
            P("wide", None, None),
        ),
        out_specs=P(("grp", "wide"), None),
        check_vma=False,
    )
```

```python
import functools
import math

import jax
import jax.numpy as jnp
from jax import lax
from jax.experimental import pallas as pl
from jax.experimental.pallas import tpu as pltpu
from jax.sharding import PartitionSpec as P


QUERY_HEADS = 32
KEY_VALUE_HEADS = 4
HEAD_SIZE = 64


score_masked_rows = -1e30


def exchanged(shard, axis, distance):
    return lax.ppermute(shard, axis, [(i, i ^ distance) for i in range(lax.axis_size(axis))])


LANES = 128


def cache_kernel(
    device_ref, lengths_ref, positions_ref, own_ref, visit_ref, row_k_ref, row_v_ref, cache_k_ref, cache_v_ref,
    own_out_ref, own_stats_ref, visit_out_ref,
    keys, values, stacked, buffer, weights, result, shifts, stats,
):
    group = pl.program_id(0)
    rows = own_ref.shape[0]
    span = cache_k_ref.shape[0]
    shared = LANES // HEAD_SIZE
    pairs = own_ref.shape[1] // LANES // shared
    key_count = keys.shape[0]
    padded = key_count - span
    lane = lax.broadcasted_iota(jnp.int32, (1, LANES), 1)
    low = lane < HEAD_SIZE

    @pl.when(group == 0)
    def _():
        device = device_ref[0]
        start = (device % 2) * span
        length = lengths_ref[device // 2]
        marked = positions_ref[pl.ds(device // 2, 1), :]
        counter = jnp.ones((marked.shape[1], LANES), jnp.bfloat16)
        step = LANES

        def mark(block, carry):
            location = start + block * step + lax.broadcasted_iota(jnp.int32, (step, 1), 0)
            equal = jnp.where(location == marked, 1.0, 0.0).astype(jnp.bfloat16)
            count = jnp.dot(equal, counter, preferred_element_type=jnp.float32)
            shut = ((count > 0.5) | (location >= length)) & (lane == 0)
            at = pl.ds(pl.multiple_of(block * step, step), step)
            keys[at, LANES:] = jnp.where(shut, score_masked_rows, 0.0).astype(jnp.bfloat16)
            return carry

        lax.fori_loop(0, span // step, mark, 0)
        beyond = lax.broadcasted_iota(jnp.int32, (padded, 1), 0) >= rows
        keys[span:, LANES:] = jnp.where(beyond & (lane == 0), score_masked_rows, 0.0).astype(jnp.bfloat16)
        values[:, LANES:] = jnp.ones((key_count, LANES), jnp.bfloat16)
        stacked[:, LANES:] = jnp.where(
            lax.broadcasted_iota(jnp.int32, (stacked.shape[0], LANES), 1) == 0, 1.0, 0.0
        ).astype(jnp.bfloat16)
        stats[...] = jnp.zeros_like(stats)
        if padded > rows:
            keys[span + rows :, :LANES] = jnp.zeros((padded - rows, LANES), jnp.bfloat16)
            values[span + rows :, :LANES] = jnp.zeros((padded - rows, LANES), jnp.bfloat16)

    keys[:span, :LANES] = cache_k_ref[...]
    values[:span, :LANES] = cache_v_ref[...]
    keys[span : span + rows, :LANES] = row_k_ref[...]
    values[span : span + rows, :LANES] = row_v_ref[...]

    scale = 1.0 / math.sqrt(HEAD_SIZE)
    for half in range(shared):
        side = lane // HEAD_SIZE == half
        for pair in range(pairs):
            columns = slice((half * pairs + pair) * LANES, (half * pairs + pair + 1) * LANES)
            for source, ref in enumerate((own_ref, visit_ref)):
                query = ref[:, columns].astype(jnp.float32) * scale
                for parity in range(2):
                    base = (((half * 2 + parity) * pairs + pair) * 2 + source) * rows
                    moved = query if parity == half else pltpu.roll(query, HEAD_SIZE, 1)
                    stacked[base : base + rows, :LANES] = jnp.where(side, moved, 0.0).astype(jnp.bfloat16)

    chunk = buffer.shape[1]
    wide = 2 * LANES

    def score(turn):
        query = stacked[turn * chunk : (turn + 1) * chunk, :]
        highest = None
        for begin in range(0, key_count, wide):
            end = min(begin + wide, key_count)
            tile = lax.dot_general(
                query, keys[begin:end, :], (((1,), (1,)), ((), ())), preferred_element_type=jnp.float32
            )
            buffer[turn % 2, :, begin:end] = tile
            for lanes in range(0, end - begin, LANES):
                part = tile[:, lanes : lanes + LANES]
                highest = part if highest is None else jnp.maximum(highest, part)
        return jnp.max(highest, axis=1, keepdims=True).astype(jnp.bfloat16).astype(jnp.float32)

    def weigh(turn, shift):
        at = slice(turn * chunk, (turn + 1) * chunk)
        shifts[at, :] = jnp.broadcast_to(shift, (chunk, LANES))
        for begin in range(0, key_count, wide):
            end = min(begin + wide, key_count)
            weights[turn % 2, :, begin:end] = jnp.exp(buffer[turn % 2, :, begin:end] - shift).astype(jnp.bfloat16)
        result[at, :] = jnp.dot(weights[turn % 2], values[...], preferred_element_type=jnp.float32)

    turns = stacked.shape[0] // chunk
    shift = score(0)
    for turn in range(turns):
        ahead = score(turn + 1) if turn + 1 < turns else None
        weigh(turn, shift)
        shift = ahead

    both = 2 * rows
    seen = stats[...]
    for place in range(shared * pairs):
        half, pair = place // pairs, place % pairs
        even = slice((half * 2 * pairs + pair) * both, (half * 2 * pairs + pair + 1) * both)
        odd = slice(((half * 2 + 1) * pairs + pair) * both, ((half * 2 + 1) * pairs + pair + 1) * both)
        left, right = result[even, :LANES], result[odd, :LANES]
        if half == 0:
            right = pltpu.roll(right, HEAD_SIZE, 1)
        else:
            left = pltpu.roll(left, HEAD_SIZE, 1)
        joined = jnp.where(low, left, right)
        own_out_ref[:, place * LANES : (place + 1) * LANES] = joined[:rows]
        column = pl.multiple_of((group * shared * pairs + place) * LANES, LANES)
        visit_out_ref[:, pl.ds(column, LANES)] = joined[rows:].astype(jnp.bfloat16)
        for parity, at in enumerate((even, odd)):
            head = (group * shared * pairs + place) * 2 + parity
            total = result[at, LANES:]
            high = total.astype(jnp.bfloat16).astype(jnp.float32)
            seen = jnp.where(lane == head, shifts[at, :], seen)
            seen = jnp.where(lane == head + 2 * QUERY_HEADS, high, seen)
            seen = jnp.where(lane == head + 3 * QUERY_HEADS, total - high, seen)
    stats[...] = seen

    @pl.when(group == pl.num_programs(0) - 1)
    def _():
        own_stats_ref[...] = stats[:rows].astype(jnp.bfloat16)
        visit_out_ref[:, visit_out_ref.shape[1] - LANES :] = stats[rows:].astype(jnp.bfloat16)


def attend_cache(device, lengths, positions, own, visit, row_key_value, key_value_cache):
    rows, width = own.shape
    span = key_value_cache.shape[0]
    key_count = span + -(-rows // LANES) * LANES
    half = KEY_VALUE_HEADS * HEAD_SIZE // LANES
    group_width = width // half
    stack = 2 * rows * (QUERY_HEADS // half)
    in_hbm = functools.partial(pltpu.with_memory_space_constraint, memory_space=pltpu.HBM)
    own, row_key_value, key_value_cache = map(in_hbm, (own, row_key_value, key_value_cache))
    lengths, positions = in_hbm(lengths), in_hbm(positions)
    return pl.pallas_call(
        cache_kernel,
        grid=(half,),
        in_specs=[
            pl.BlockSpec(memory_space=pltpu.SMEM),
            pl.BlockSpec(memory_space=pltpu.SMEM),
            pl.BlockSpec(positions.shape, lambda g: (0, 0)),
            pl.BlockSpec((rows, group_width), lambda g: (0, g)),
            pl.BlockSpec((rows, group_width), lambda g: (0, g)),
            pl.BlockSpec((rows, LANES), lambda g: (0, g)),
            pl.BlockSpec((rows, LANES), lambda g: (0, half + g)),
            pl.BlockSpec((span, LANES), lambda g: (0, g)),
            pl.BlockSpec((span, LANES), lambda g: (0, half + g)),
        ],
        out_specs=[
            pl.BlockSpec((rows, group_width), lambda g: (0, g)),
            pl.BlockSpec((rows, LANES), lambda g: (0, 0)),
            pl.BlockSpec((rows, width + LANES), lambda g: (0, 0)),
        ],
        out_shape=[
            jax.ShapeDtypeStruct((rows, width), jnp.float32),
            jax.ShapeDtypeStruct((rows, LANES), jnp.bfloat16),
            jax.ShapeDtypeStruct((rows, width + LANES), jnp.bfloat16),
        ],
        scratch_shapes=[
            pltpu.VMEM((key_count, 2 * LANES), jnp.bfloat16),
            pltpu.VMEM((key_count, 2 * LANES), jnp.bfloat16),
            pltpu.VMEM((stack, 2 * LANES), jnp.bfloat16),
            pltpu.VMEM((2, 4 * rows, key_count), jnp.float32),
            pltpu.VMEM((2, 4 * rows, key_count), jnp.bfloat16),
            pltpu.VMEM((stack, 2 * LANES), jnp.float32),
            pltpu.VMEM((stack, LANES), jnp.float32),
            pltpu.VMEM((2 * rows, LANES), jnp.float32),
        ],
        compiler_params=pltpu.CompilerParams(vmem_limit_bytes=20 << 20),
        name="cache_attention",
    )(
        device.reshape(1), lengths, positions, own, visit,
        row_key_value, row_key_value, key_value_cache, key_value_cache,
    )


def merge_kernel(own_ref, own_stats_ref, far_ref, resid_ref, gain_ref, shares_ref, payload_ref, residual_ref):
    width = own_ref.shape[1]
    far_stats = far_ref[:, width:]
    head_of = lax.broadcasted_iota(jnp.int32, (LANES, width), 1) // HEAD_SIZE
    stat = lax.broadcasted_iota(jnp.int32, (LANES, width), 0)

    def spread(stats):
        pick_shift = jnp.where(stat == head_of, 1.0, 0.0).astype(jnp.bfloat16)
        pick_total = jnp.where(
            (stat == head_of + 2 * QUERY_HEADS) | (stat == head_of + 3 * QUERY_HEADS), 1.0, 0.0
        ).astype(jnp.bfloat16)
        return (
            jnp.dot(stats, pick_shift, preferred_element_type=jnp.float32),
            jnp.dot(stats, pick_total, preferred_element_type=jnp.float32),
        )

    own_shift, own_total = spread(own_stats_ref[...])
    far_shift, far_total = spread(far_stats)
    joint = jnp.maximum(own_shift, far_shift)
    own_scale = jnp.exp(own_shift - joint)
    far_scale = jnp.exp(far_shift - joint)
    merged = own_ref[...] * own_scale + far_ref[:, :width].astype(jnp.float32) * far_scale
    total = own_total * own_scale + far_total * far_scale
    attn = (merged / total).astype(jnp.bfloat16).astype(jnp.float32)
    residual = resid_ref[...].astype(jnp.float32) + attn
    residual_ref[...] = residual
    power = jnp.mean(residual * residual, axis=1, keepdims=True)
    normed = residual * lax.rsqrt(power + 1e-06) * gain_ref[...]
    payload_ref[:, :width] = normed.astype(jnp.bfloat16)
    payload_ref[:, width:] = shares_ref[...]


def merge(own, own_stats, far, resid, norm_gain, shares):
    rows, width = own.shape
    return pl.pallas_call(
        merge_kernel,
        out_shape=[
            jax.ShapeDtypeStruct((rows, width + shares.shape[1]), jnp.bfloat16),
            jax.ShapeDtypeStruct((rows, width), jnp.float32),
        ],
        compiler_params=pltpu.CompilerParams(vmem_limit_bytes=12 << 20),
        name="merge_norm",
    )(own, own_stats, far, resid, norm_gain.reshape(1, width), shares)


def expert_kernel(device_ref, near_ref, far_ref, gate_ref, up_ref, down_ref, keep_ref, send_ref, *, experts):
    depth = gate_ref.shape[1]
    hidden_width = gate_ref.shape[2]
    rows = jnp.concatenate([near_ref[...], far_ref[...]], axis=0)
    device = device_ref[0]
    column = lax.broadcasted_iota(jnp.int32, (1, rows.shape[1] - depth), 1)
    own_column = (column == device) | (column == device + experts)
    share = jnp.sum(
        jnp.where(own_column, rows[:, depth:].astype(jnp.float32), 0.0), axis=1, keepdims=True
    )
    rows = rows[:, :depth]
    step = 256
    hidden = []
    for begin in range(0, hidden_width, step):
        at = slice(begin, min(begin + step, hidden_width))
        gate_act = jnp.dot(rows, gate_ref[0, :, at], preferred_element_type=jnp.float32)
        up_act = jnp.dot(rows, up_ref[0, :, at], preferred_element_type=jnp.float32)
        hidden.append((jax.nn.silu(gate_act) * up_act).astype(jnp.bfloat16))
    hidden = jnp.concatenate(hidden, axis=1)
    kept = keep_ref.shape[0]
    step = 512
    for begin in range(0, depth, step):
        at = slice(begin, min(begin + step, depth))
        expert_out = jnp.dot(hidden, down_ref[0, :, at], preferred_element_type=jnp.float32)
        partial = share * expert_out.astype(jnp.bfloat16).astype(jnp.float32)
        keep_ref[:, at] = partial[:kept]
        send_ref[:, at] = partial[kept:].astype(jnp.bfloat16)


def expert(device, near, far, w_gate, w_up, w_down, experts):
    rows = near.shape[0]
    depth = w_gate.shape[1]
    return pl.pallas_call(
        functools.partial(expert_kernel, experts=experts),
        in_specs=[pl.BlockSpec(memory_space=pltpu.SMEM)] + [pl.BlockSpec(memory_space=pltpu.VMEM)] * 5,
        out_specs=[pl.BlockSpec(memory_space=pltpu.VMEM)] * 2,
        out_shape=[
            jax.ShapeDtypeStruct((rows, depth), jnp.float32),
            jax.ShapeDtypeStruct((rows, depth), jnp.bfloat16),
        ],
        compiler_params=pltpu.CompilerParams(vmem_limit_bytes=20 << 20),
        name="expert",
    )(device.reshape(1), near, far, w_gate, w_up, w_down)


def local(
    query_rows,
    row_key_value,
    key_value_cache,
    resid,
    norm_gain,
    lengths,
    positions,
    expert_ids,
    gate_scores,
    w_gate,
    w_up,
    w_down,
):
    masked_row_count, _ = resid.shape
    device = lax.axis_index("wide")
    experts = lax.axis_size("wide")
    mix = gate_scores / jnp.sum(gate_scores, axis=-1, keepdims=True)
    shares = jnp.sum(
        jnp.where(expert_ids[..., None] == jnp.arange(experts, dtype=jnp.int32), mix[..., None], 0.0), axis=1
    )
    shares_high = shares.astype(jnp.bfloat16)
    shares_low = (shares - shares_high.astype(jnp.float32)).astype(jnp.bfloat16)
    tail = -(-2 * experts // LANES) * LANES
    filler = jnp.zeros((masked_row_count, tail - 2 * experts), jnp.bfloat16)
    shares = jnp.concatenate([shares_high, shares_low, filler], axis=1)
    visitor = exchanged(query_rows, "wide", 1)
    own, own_stats, hosted = attend_cache(
        device, lengths, positions, query_rows, visitor, row_key_value, key_value_cache
    )
    far = exchanged(hosted, "wide", 1)
    payload, residual = merge(own, own_stats, far, resid, norm_gain, shares)
    planes = experts // 4
    blocks = [payload]
    total = residual
    beside, near, far = [], [None] * planes, [None] * planes
    for k in range(1, planes):
        low_bit = k & -k
        blocks.append(exchanged(blocks[k - low_bit], "wide", 4 * low_bit))
    for k in range(planes):
        low_bit = k & -k
        if k > low_bit:
            beside.append(exchanged(beside[k - low_bit], "wide", 4 * low_bit))
        else:
            beside.append(exchanged(blocks[k], "wide", 2))
        near[k] = jnp.concatenate([blocks[k], beside[k]], axis=0)
        far[k] = exchanged(near[k], "wide", 1)
    for k in range(planes):
        kept, sent = expert(device, near[k], far[k], w_gate, w_up, w_down, experts)
        sent = exchanged(sent, "wide", 1)
        half = kept + sent.astype(jnp.float32)
        mine, other = half[:masked_row_count], half[masked_row_count:].astype(jnp.bfloat16)
        other = exchanged(other, "wide", 2)
        mine = mine + other.astype(jnp.float32)
        if k % 2 == 0 and k:
            relayed = exchanged(mine.astype(jnp.bfloat16), "wide", 4).astype(jnp.float32)
            continue
        if k > 1:
            mine = mine + relayed
        if k:
            mine = exchanged(mine.astype(jnp.bfloat16), "wide", 4 * k).astype(jnp.float32)
        total = total + mine
    return total.astype(jnp.bfloat16)


def solution(mesh):
    return jax.shard_map(
        local,
        mesh=mesh,
        in_specs=(
            P(("grp", "wide"), None),
            P(("grp", "wide"), None),
            P(("grp", "wide"), None),
            P(("grp", "wide"), None),
            P(),
            P("grp"),
            P("grp", None),
            P(("grp", "wide"), None),
            P(("grp", "wide"), None),
            P("wide", None, None),
            P("wide", None, None),
            P("wide", None, None),
        ),
        out_specs=P(("grp", "wide"), None),
        check_vma=False,
    )
```
